128 devices in a mesh: off: 4 (over z_hi, core), img: 32 (over x, y, z_lo).
Axes of the slice: x: 4, y: 4, z: 4 (z_hi: 2, z_lo: 2; z = z_hi * 2 + z_lo), core: 2. Of those that a mesh axis runs over, the one named last changes fastest.
Arguments:
- shot_traces: bfloat16 [4, 32, 32, 4096], P('off', None, 'img'), may hold values from -6 to 6
- assign: int32 [32, 32, 4], P('off', 'img'), may hold values from 0 to 3, each once within a row
- aperture: int32 [32, 32], P('off', 'img'), may hold values from 0 to 1
- band: int32 [32, 1024], P('off', 'img'), may hold values from 0 to 3584
- interp: bfloat16 [1024, 512, 64], P('img'), may hold values from -0.25 to 0.25
- amp: bfloat16 [1024, 128, 128], P('img'), may hold values from -0.5 to 0.5
Outputs:
- image: float32 [64, 131072], P('off', 'img')
The draws below stay inside these ranges and needn't reach their ends.
All inputs are finite; a program needn't handle non-finite values.
Results may differ from the reference program's by a relative error of at most 0.0065.
Values may be sent and summed in bfloat16 or wider, within the bound.
No kernel may reach another device: no remote copies, remote signals or barrier semaphores. Data moves between devices by JAX's collectives and lax.ppermute only.
A program may use at most 128 MiB of HBM per device.

```python
import math
import jax
import jax.numpy as jnp
from jax import lax

NT = 4096
WIN = 512
DZ = 64
PG = 128
NG = 32
NB = 32
NSHOT = 4
TR_DEV = 4
TRB = 128
N_IMG = 32


def draw_aperture(key, part):
    key_counts = jax.random.fold_in(key, 11)
    key_ranks = jax.random.fold_in(key, 12)
    counts = jax.random.randint(key_counts, (N_IMG,), 1, NB + 1)
    ranks = jax.random.randint(key_ranks, (NB, N_IMG), 0, NB)
    return (ranks < counts[None, :]).astype(jnp.int32)


def set_ends(entries, rng, smallest, high):
    longest = entries.shape.index(max(entries.shape))
    spots = []
    for shift in (0, 1):
        where = [jax.random.randint(jax.random.fold_in(rng, axis), (), 0, length) for axis, length in enumerate(entries.shape)]
        where[longest] = (where[longest] + shift) % entries.shape[longest]
        spots.append(tuple(where))
    return entries.at[spots[0]].set(smallest).at[spots[1]].set(high)


def block_levels(own_key, extent, split, low, largest):
    def one(dim, blocks):
        steps = jax.random.uniform(jax.random.fold_in(jax.random.fold_in(own_key, 6), dim), (blocks,), jnp.float32, low / len(split), largest / len(split))
        return jnp.repeat(jnp.exp(steps), extent[dim] // blocks).reshape((-1,) + (1,) * (len(extent) - dim - 1))

    factor_of = one(*split[0])
    for cut in split[1:]:
        factor_of = factor_of * one(*cut)
    return factor_of


def noise(key, extent, width, reach, pieces=(), held_as=jnp.bfloat16):
    result = jax.random.normal(key, extent, jnp.float32) * width
    if len(pieces) > 0:
        result = block_levels(key, extent, pieces, -0.22, 0.18) * result
    return jnp.clip(result, min=-reach, max=reach).astype(held_as)


def setup_inputs(seed: int = 0) -> dict:
    splits = jax.random.split(jax.random.key(seed), 7)
    return {
        "shot_traces": noise(splits[0], (NSHOT, NB, N_IMG, NT), 1.0, 6.0, ((0, 4), (2, 32))),
        "assign": jax.vmap(lambda own: jax.random.permutation(own, TR_DEV))(jax.random.split(splits[1], NB * N_IMG)).reshape((NB, N_IMG, TR_DEV)).astype(jnp.int32),
        "aperture": draw_aperture(jax.random.fold_in(splits[6], 71), 0),
        "band": set_ends(jax.random.randint(splits[3], (NB, N_IMG * NG), 0, NT - WIN + 1), jax.random.fold_in(splits[3], 1), 0, NT - WIN).astype(jnp.int32),
        "interp": noise(splits[4], (N_IMG * NG, WIN, DZ), WIN ** -0.5, 0.25, ((0, 32),)),
        "amp": noise(splits[5], (N_IMG * NG, TRB, PG), TRB ** -0.5, 0.5, ((0, 32),)),
    }


def filter_traces(raw_traces):
    widened = raw_traces.astype(jnp.float32)
    earlier = jnp.concatenate([jnp.zeros_like(widened[..., :1]), widened[..., :-1]], axis=-1)
    return (widened - 0.9 * earlier).astype(jnp.bfloat16)

def reference(shot_traces, assign, aperture, band, interp, amp):
    filtered = filter_traces(shot_traces)
    received = jnp.transpose(filtered, (1, 2, 0, 3))
    picked = jnp.take_along_axis(received, assign[..., None].astype(jnp.int32), axis=2)
    block_traces = picked.reshape(NB, TRB, NT)
    tile_interp = interp.reshape(N_IMG, NG, WIN, DZ)
    tile_amp = amp.reshape(N_IMG, NG, TRB, PG)
    tile_band = jnp.transpose(band.reshape(NB, N_IMG, NG), (1, 0, 2))
    tile_aperture = jnp.transpose(aperture, (1, 0))

    def one_tile(packed):
        interp_here, amp_here, band_here, flags_here = packed

        def one_block(running, inputs):
            traces_here, starts, flag = inputs
            windows = jax.vmap(lambda first: lax.dynamic_slice_in_dim(traces_here, first, WIN, axis=1))(starts)
            depthrows = jnp.einsum('gtw,gwz->gzt', windows.astype(jnp.float32), interp_here.astype(jnp.float32)).astype(jnp.bfloat16)
            return (running + flag.astype(jnp.float32) * depthrows.astype(jnp.float32), None)
        start_stack = jnp.zeros((NG, DZ, TRB), jnp.float32)
        stacked, unused = lax.scan(one_block, start_stack, (block_traces, band_here, flags_here))
        finished = jnp.einsum('gzt,gtp->zgp', stacked, amp_here.astype(jnp.float32), precision=lax.Precision.HIGHEST)
        return finished.reshape(DZ, NG * PG)
    tiles = lax.map(one_tile, (tile_interp, tile_amp, tile_band, tile_aperture))
    scale = jnp.float32(1.0 / math.sqrt(NB))
    return jnp.transpose(tiles, (1, 0, 2)).reshape(DZ, N_IMG * NG * PG) * scale
```

```python
import functools
import math

import jax
import jax.numpy as jnp
from jax import lax
from jax.experimental import pallas as pl
from jax.experimental.pallas import tpu as pltpu
from jax.sharding import Mesh, PartitionSpec as P

LANES = 128
SUB = 8
OFF = ("zh", "core")
RING = ("zh", "zl")
PLANE = ("x", "y")
IMG = ("x", "y", "zl")
EVERY = OFF + IMG


def stack_kernel(core_ref, assign_ref, meta_ref, traces_ref, out_ref, rows_ref, list_ref, *, blocks, chunks, per_off, tiles, groups, window):
    slots = SUB
    pitch = (chunks + 1) * slots
    core = core_ref[0]
    lane = lax.broadcasted_iota(jnp.int32, (slots, LANES), 1)
    parts = window // LANES

    def place(block, carry):
        owner = block // per_off
        within = block % per_off
        for slot in range(slots):
            half = slot // 4
            held = ((owner % 2) ^ core) * 4 + (owner // 2) * 2 + half
            shot = assign_ref[held, within * 4 + slot % 4]
            source = ((shot % 2) ^ core) * 4 + (shot // 2) * 2 + half
            rows_ref[pl.ds(block * pitch + slot, chunks, stride=slots), :] = traces_ref[source, block].astype(jnp.float32)
        return carry

    lax.fori_loop(0, blocks, place, 0)

    def one_tile(tile, carry):
        def note(block, count):
            list_ref[count] = block
            return count + meta_ref[(block // per_off) * tiles + tile, per_off * groups + block % per_off]

        count = lax.fori_loop(0, blocks, note, 0, unroll=True)

        def add(step, sums):
            block = list_ref[step]
            row = (block // per_off) * tiles + tile
            column = (block % per_off) * groups
            result = []
            for group in range(groups):
                first = meta_ref[row, column + group]
                shift = first % LANES
                base = pl.multiple_of(block * pitch + (first // LANES) * slots, slots)
                mask = lane >= shift
                back = (LANES - shift) % LANES
                piece = rows_ref[pl.ds(base, (parts + 1) * slots), :]
                for part in range(parts):
                    mixed = jnp.where(mask, piece[part * slots : (part + 1) * slots], piece[(part + 1) * slots : (part + 2) * slots])
                    result.append(sums[group * parts + part] + pltpu.roll(mixed, back, 1))
            return tuple(result)

        zero = tuple(jnp.zeros((slots, LANES), jnp.float32) for _ in range(groups * parts))
        sums = lax.fori_loop(0, count, add, zero)
        for group in range(groups):
            for part in range(parts):
                out_ref[tile, group, :, part * LANES : (part + 1) * LANES] = sums[group * parts + part].astype(jnp.bfloat16)
        return carry

    lax.fori_loop(0, tiles, one_tile, 0)


def image_kernel(first_ref, stacked_ref, interp_ref, amp_ref, out_ref, *, scale):
    sources, _, slots, window = stacked_ref.shape
    stacked = stacked_ref[...].reshape(sources * slots, window)
    depth = lax.dot_general(interp_ref[0], stacked, (((1,), (1,)), ((), ())), preferred_element_type=jnp.float32)
    high = depth.astype(jnp.bfloat16)
    low = (depth - high.astype(jnp.float32)).astype(jnp.bfloat16)
    amp = amp_ref[0]
    image = jnp.dot(high, amp, preferred_element_type=jnp.float32) + jnp.dot(low, amp, preferred_element_type=jnp.float32)
    out_ref[...] = (image * scale).reshape(out_ref.shape)


def local(shot_traces, assign, aperture, band, interp, amp):
    blocks, samples = shot_traces.shape[1], shot_traces.shape[3]
    per_off, all_groups = band.shape
    offs = blocks // per_off
    groups = all_groups // offs
    tiles = lax.axis_size("x") * lax.axis_size("y")
    window, depth = interp.shape[1], interp.shape[2]
    traces, pixels = amp.shape[1], amp.shape[2]
    chunks = samples // LANES
    core = lax.axis_index("core")
    off = lax.axis_index(OFF)

    mine = jnp.transpose(band.reshape(per_off, offs, groups), (1, 0, 2)).reshape(offs, per_off * groups)
    flags = jnp.broadcast_to(aperture[:, 0][None, :], (offs, per_off))
    row = jnp.concatenate([mine, flags], axis=1)
    row = jnp.pad(row, ((0, 0), (0, LANES - row.shape[1])))
    row = jnp.broadcast_to(row[:, None, :], (offs, tiles, LANES)).reshape(offs * tiles, LANES)
    meta = lax.all_to_all(row, OFF + PLANE, 0, 0, tiled=True)

    widened = shot_traces[0, :, 0, :].astype(jnp.float32)
    earlier = jnp.concatenate([jnp.zeros_like(widened[:, :1]), widened[:, :-1]], axis=-1)
    filtered = (widened - 0.9 * earlier).astype(jnp.bfloat16).reshape(blocks, chunks, LANES)
    codes = assign.reshape(1, per_off * assign.shape[2]).astype(jnp.bfloat16)
    codes = jnp.pad(codes, ((0, chunks - 1), (0, LANES - codes.shape[1])))
    sent = jnp.concatenate([filtered, codes[None]], axis=0)
    ring = lax.axis_size("zh") * lax.axis_size("zl")
    column = lax.all_to_all(jnp.broadcast_to(sent[None], (ring,) + sent.shape), RING, 0, 0, tiled=True)
    other = lax.ppermute(column, "core", [(0, 1), (1, 0)])
    both = jnp.concatenate([column, other], axis=0)
    slots_from = both[:, blocks, 0, :].astype(jnp.int32)

    smem = pl.BlockSpec(memory_space=pltpu.SMEM)
    vmem = pl.BlockSpec(memory_space=pltpu.VMEM)
    stacked = pl.pallas_call(
        functools.partial(stack_kernel, blocks=blocks, chunks=chunks, per_off=per_off, tiles=tiles, groups=groups, window=window),
        out_shape=jax.ShapeDtypeStruct((tiles, groups, SUB, window), jnp.bfloat16),
        in_specs=[smem, smem, smem, vmem],
        out_specs=vmem,
        scratch_shapes=[
            pltpu.VMEM((blocks * (chunks + 1) * SUB, LANES), jnp.float32),
            pltpu.SMEM((blocks,), jnp.int32),
        ],
        name="stack_windows",
    )(core.reshape(1), slots_from, meta, both)

    arrived = lax.all_to_all(stacked, PLANE, 0, 0, tiled=True)

    image = pl.pallas_call(
        functools.partial(image_kernel, scale=1.0 / math.sqrt(blocks)),
        out_shape=jax.ShapeDtypeStruct((offs, depth // offs, groups * pixels), jnp.float32),
        grid_spec=pltpu.PrefetchScalarGridSpec(
            num_scalar_prefetch=1,
            grid=(groups,),
            in_specs=[
                pl.BlockSpec((tiles, 1, SUB, window), lambda g, first: (0, g, 0, 0)),
                pl.BlockSpec((1, depth, window), lambda g, first: (first[0] + g, 0, 0)),
                pl.BlockSpec((1, traces, pixels), lambda g, first: (first[0] + g, 0, 0)),
            ],
            out_specs=pl.BlockSpec((offs, depth // offs, pixels), lambda g, first: (0, 0, g)),
        ),
        name="image_groups",
    )((off * groups).reshape(1), arrived, jnp.swapaxes(interp, 1, 2), amp)

    rows = lax.all_to_all(image, OFF, 0, 0, tiled=True)
    return jnp.transpose(rows, (1, 0, 2)).reshape(depth // offs, offs * groups * pixels)


def solution(mesh):
    fine = Mesh(mesh.devices.reshape(2, 2, 4, 4, 2), EVERY)
    placed = (
        P(OFF, None, IMG, None),
        P(OFF, IMG, None),
        P(OFF, IMG),
        P(OFF, IMG),
        P(IMG, None, None),
        P(IMG, None, None),
    )
    return jax.shard_map(local, mesh=fine, in_specs=placed, out_specs=P(OFF, IMG), check_vma=False)
```

```python
import functools
import math

import jax
import jax.numpy as jnp
from jax import lax
from jax.experimental import pallas as pl
from jax.experimental.pallas import tpu as pltpu
from jax.sharding import Mesh, PartitionSpec as P

LANES = 128
SUB = 8
OFF = ("zh", "core")
PLANE = ("x", "y")
IMG = ("x", "y", "zl")
EVERY = OFF + IMG
LIST_SHIFT = 13


def stack_kernel(at_ref, codes_ref, meta_ref, *refs, pieces, blocks, chunks, per_off, tiles, groups, window):
    piece_refs = refs[:pieces]
    out_ref, traces_ref, rows_ref, list_ref, sems = refs[pieces:]
    slots = SUB
    pitch = (chunks + 1) * slots
    parts = window // LANES
    copies = [
        pltpu.make_async_copy(piece_refs[piece], traces_ref.at[at_ref[piece]], sems.at[piece]) for piece in range(pieces)
    ]
    for copy in copies:
        copy.start()
    lane = lax.broadcasted_iota(jnp.int32, (slots, LANES), 1)
    rows_ref[pl.ds(blocks * pitch, pitch), :] = jnp.zeros((pitch, LANES), jnp.float32)
    for copy in copies:
        copy.wait()

    for owner in range(blocks // per_off):
        held = [at_ref[pieces + owner * 2 + half] * LANES for half in range(2)]

        def place(within, carry, owner=owner, held=held):
            block = owner * per_off + within
            for slot in range(slots):
                source = codes_ref[held[slot // 4] + within * 4 + slot % 4] * 2 + slot // 4
                rows_ref[pl.ds(block * pitch + slot, chunks, stride=slots), :] = traces_ref[source, block].astype(jnp.float32)
            return carry

        lax.fori_loop(0, per_off, place, 0)

    def one_tile(tile, carry):
        count = 0
        for block in range(blocks):
            row = ((block // per_off) * tiles + tile) * LANES
            within = block % per_off
            list_ref[count] = row + (block * pitch * (1 << LIST_SHIFT) + within * groups)
            count = count + meta_ref[row + per_off * groups + within]
        list_ref[count] = blocks * pitch * (1 << LIST_SHIFT)

        def add(step, sums):
            sums = list(sums)
            for turn in range(2):
                code = list_ref[2 * step + turn]
                start = code >> LIST_SHIFT
                entry = code & ((1 << LIST_SHIFT) - 1)
                for group in range(groups):
                    first = meta_ref[entry + group]
                    shift = first & (LANES - 1)
                    base = pl.multiple_of(start + ((first >> 7) << 3), slots)
                    mask = lane >= shift
                    piece = rows_ref[pl.ds(base, (parts + 1) * slots), :]
                    for part in range(parts):
                        mixed = jnp.where(mask, piece[part * slots : (part + 1) * slots], piece[(part + 1) * slots : (part + 2) * slots])
                        sums[group * parts + part] += pltpu.roll(mixed, LANES - shift, 1)
            return tuple(sums)

        zero = tuple(jnp.zeros((slots, LANES), jnp.float32) for _ in range(groups * parts))
        sums = lax.fori_loop(0, (count + 1) >> 1, add, zero)
        for group in range(groups):
            for part in range(parts):
                out_ref[tile, group, :, part * LANES : (part + 1) * LANES] = sums[group * parts + part].astype(jnp.bfloat16)
        return carry

    lax.fori_loop(0, tiles, one_tile, 0)


def image_kernel(place_ref, stacked_ref, interp_ref, amp_ref, out_ref, *, scale):
    sources, groups, slots, window = stacked_ref.shape
    offs, rows, pixels = out_ref.shape
    pixels = pixels // groups
    for group in range(groups):
        stacked = stacked_ref[:, group].reshape(sources * slots, window)
        depth = lax.dot_general(interp_ref[group], stacked, (((1,), (1,)), ((), ())), preferred_element_type=jnp.float32)
        high = depth.astype(jnp.bfloat16)
        low = (depth - high.astype(jnp.float32)).astype(jnp.bfloat16)
        amp = amp_ref[group]
        image = jnp.dot(high, amp, preferred_element_type=jnp.float32) + jnp.dot(low, amp, preferred_element_type=jnp.float32)
        image = (image * scale).astype(out_ref.dtype)
        for off in range(offs):
            out_ref[place_ref[off], :, group * pixels : (group + 1) * pixels] = image[off * rows : (off + 1) * rows]


def join_kernel(place_ref, *refs):
    out_ref = refs[-1]
    for index, ref in enumerate(refs[:-1]):
        width = ref.shape[1]
        out_ref[:, pl.ds(pl.multiple_of(place_ref[index] * width, LANES), width)] = ref[...].astype(out_ref.dtype)


def ring_pairs(step):
    return [(z, (z + step) % 4) for z in range(4)]


def local(shot_traces, assign, aperture, band, interp, amp):
    blocks, samples = shot_traces.shape[1], shot_traces.shape[3]
    per_off, all_groups = band.shape
    offs = blocks // per_off
    groups = all_groups // offs
    tiles = lax.axis_size("x") * lax.axis_size("y")
    window, depth = interp.shape[1], interp.shape[2]
    pixels = amp.shape[2]
    chunks = samples // LANES
    zh, core, zl = lax.axis_index("zh"), lax.axis_index("core"), lax.axis_index("zl")
    z = zh * 2 + zl
    off = zh * 2 + core
    swap = [(0, 1), (1, 0)]

    widened = shot_traces[0, :, 0, :].astype(jnp.float32)
    earlier = jnp.concatenate([jnp.zeros_like(widened[:, :1]), widened[:, :-1]], axis=-1)
    filtered = (widened - 0.9 * earlier).astype(jnp.bfloat16).reshape(blocks, chunks, LANES)
    codes = assign.reshape(1, per_off * assign.shape[2]).astype(jnp.bfloat16)
    codes = jnp.pad(codes, ((0, chunks - 1), (0, LANES - codes.shape[1])))
    sent = jnp.concatenate([filtered, codes[None]], axis=0)
    steps = (1, 3, 2)
    ring = [lax.ppermute(sent, ("zh", "zl"), ring_pairs(step)) for step in steps]

    mine = jnp.transpose(band.reshape(per_off, offs, groups), (1, 0, 2)).reshape(offs, per_off * groups)
    flags = jnp.broadcast_to(aperture[:, 0][None, :], (offs, per_off))
    row = jnp.concatenate([mine, flags], axis=1)
    row = jnp.pad(row, ((0, 0), (0, LANES - row.shape[1])))
    row = jnp.broadcast_to(row[:, None, :], (offs, tiles, LANES)).reshape(offs * tiles, LANES)
    meta = lax.all_to_all(row, OFF + PLANE, 0, 0, tiled=True)

    *ring, meta = lax.optimization_barrier((*ring, meta))
    column = [sent, *ring]
    pieces = column + [lax.ppermute(piece, "core", swap) for piece in column]
    held = jnp.stack([piece[blocks, 0] for piece in pieces]).astype(jnp.int32).reshape(len(pieces) * LANES)

    at = [None] * len(pieces)
    where = [0] * len(pieces)
    for turn in range(2):
        for index, step in enumerate((0,) + steps):
            from_z = (z - step) % 4
            spot = (from_z // 2) * 4 + (core ^ turn) * 2 + from_z % 2
            at[turn * 4 + index] = spot
            for want in range(len(pieces)):
                where[want] = where[want] + jnp.where(spot == want, turn * 4 + index, 0)
    at = jnp.stack(at + where).astype(jnp.int32)

    smem = pl.BlockSpec(memory_space=pltpu.SMEM)
    vmem = pl.BlockSpec(memory_space=pltpu.VMEM)
    anywhere = pl.BlockSpec(memory_space=pl.ANY)
    stacked = pl.pallas_call(
        functools.partial(
            stack_kernel, pieces=len(pieces), blocks=blocks, chunks=chunks, per_off=per_off, tiles=tiles, groups=groups, window=window
        ),
        out_shape=jax.ShapeDtypeStruct((tiles, groups, SUB, window), jnp.bfloat16),
        in_specs=[smem, smem, smem] + [anywhere] * len(pieces),
        out_specs=vmem,
        scratch_shapes=[
            pltpu.VMEM((len(pieces), blocks + 1, chunks, LANES), jnp.bfloat16),
            pltpu.VMEM(((blocks + 1) * (chunks + 1) * SUB, LANES), jnp.float32),
            pltpu.SMEM((blocks + 1,), jnp.int32),
            pltpu.SemaphoreType.DMA((len(pieces),)),
        ],
        name="stack_windows",
    )(at, held, meta.reshape(-1), *pieces)

    arrived = lax.all_to_all(stacked, PLANE, 0, 0, tiled=True)

    interp_here = lax.dynamic_slice_in_dim(jnp.swapaxes(interp, 1, 2), off * groups, groups, 0)
    amp_here = lax.dynamic_slice_in_dim(amp, off * groups, groups, 0)
    place = jnp.stack([((d // 2) ^ zh) * 2 + ((d % 2) ^ core) for d in range(offs)]).astype(jnp.int32)
    image = pl.pallas_call(
        functools.partial(image_kernel, scale=1.0 / math.sqrt(blocks)),
        out_shape=jax.ShapeDtypeStruct((offs, depth // offs, groups * pixels), jnp.bfloat16),
        in_specs=[smem, vmem, vmem, vmem],
        out_specs=vmem,
        name="image_groups",
    )(place, arrived, interp_here, amp_here)

    image = image.reshape(2, 2, depth // offs, groups * pixels)
    beside = lax.ppermute(image[:, 1], "core", swap)
    far_own = lax.ppermute(image[1, 0], "zh", swap)
    far_beside = lax.ppermute(beside[1], "zh", swap)
    order = jnp.stack([off, off ^ 1, off ^ 2, off ^ 3]).astype(jnp.int32)
    return pl.pallas_call(
        join_kernel,
        out_shape=jax.ShapeDtypeStruct((depth // offs, offs * groups * pixels), jnp.float32),
        in_specs=[smem] + [vmem] * 4,
        out_specs=vmem,
        name="join_groups",
    )(order, image[0, 0], beside[0], far_own, far_beside)


def solution(mesh):
    fine = Mesh(mesh.devices.reshape(2, 2, 4, 4, 2), EVERY)
    placed = (
        P(OFF, None, IMG, None),
        P(OFF, IMG, None),
        P(OFF, IMG),
        P(OFF, IMG),
        P(IMG, None, None),
        P(IMG, None, None),
    )
    return jax.shard_map(local, mesh=fine, in_specs=placed, out_specs=P(OFF, IMG), check_vma=False)
```

```python
import functools
import math

import jax
import jax.numpy as jnp
from jax import lax
from jax.experimental import pallas as pl
from jax.experimental.pallas import tpu as pltpu
from jax.sharding import Mesh, PartitionSpec as P

LANES = 128
SUB = 8
OFF = ("zh", "core")
PLANE = ("x", "y")
IMG = ("x", "y", "zl")
EVERY = OFF + IMG
CODE_SHIFT = 7
TURNS = 8
MASK = jnp.int16


def in_vmem(array):
    return pltpu.with_memory_space_constraint(array, pltpu.VMEM)


def prepare_kernel(off_ref, assign_ref, band_ref, aperture_ref, traces_ref, out_ref, meta_ref, rows_ref, *, offs, pitch):
    blocks, samples = traces_ref.shape
    chunks = samples // LANES
    lane = lax.broadcasted_iota(jnp.int32, (blocks, LANES), 1)
    before = jnp.zeros((blocks, LANES), jnp.float32)
    for chunk in range(chunks):
        here = traces_ref[:, chunk * LANES : (chunk + 1) * LANES].astype(jnp.float32)
        turned = pltpu.roll(here, 1, 1)
        rows_ref[pl.ds(chunk, blocks, stride=chunks), :] = here - 0.9 * jnp.where(lane == 0, before, turned)
        before = turned
    for block in range(blocks):
        out_ref[block] = rows_ref[block * chunks : (block + 1) * chunks].astype(out_ref.dtype)
    slots, owned = assign_ref.shape
    spot = lax.broadcasted_iota(jnp.int32, (chunks, LANES), 1)
    codes = jnp.zeros((chunks, LANES), jnp.float32)
    for slot in range(slots):
        for within in range(owned):
            codes = jnp.where(spot == slot * owned + within, assign_ref[slot, within].astype(jnp.float32), codes)
    out_ref[blocks] = codes.astype(out_ref.dtype)
    groups = band_ref.shape[1] // offs
    tiles = meta_ref.shape[0] // offs
    spot = lax.broadcasted_iota(jnp.int32, (SUB, LANES), 1)
    here = (off_ref[0] * owned + (spot // groups)) * pitch
    flags = jnp.full((SUB, LANES), (offs * owned * pitch) << CODE_SHIFT, jnp.int32)
    for within in range(owned):
        flags = jnp.where(spot == owned * groups + within, aperture_ref[0, within], flags)
    for owner in range(offs):
        first = jnp.zeros((SUB, LANES), jnp.int32)
        for within in range(owned):
            for group in range(groups):
                first = jnp.where(spot == within * groups + group, band_ref[within, owner * groups + group], first)
        code = ((here + (first >> 7)) << CODE_SHIFT) | ((-first) & (LANES - 1))
        row = jnp.where(spot < owned * groups, code, flags)
        for tile in range(0, tiles, SUB):
            meta_ref[owner * tiles + tile : owner * tiles + tile + SUB] = row


def stack_kernel(at_ref, meta_ref, *refs, pieces, blocks, chunks, per_off, tiles, groups, window):
    piece_refs = refs[:pieces]
    out_ref, sums_ref, traces_ref, rows_ref, pairs_ref, words_ref, codes_ref, list_ref, sems, out_sems = refs[pieces:]
    slots = SUB
    parts = window // LANES
    halves = parts // 2
    pitch = chunks - halves + 1
    for piece in range(pieces):
        words_ref[piece : piece + 1] = piece_refs[piece][blocks, 0:1, :].astype(jnp.float32).astype(jnp.int32)
    fetch = pltpu.make_async_copy(words_ref, codes_ref, sems.at[pieces])
    fetch.start()
    copies = [
        pltpu.make_async_copy(piece_refs[piece], traces_ref.at[at_ref[piece]], sems.at[piece]) for piece in range(pieces)
    ]
    for copy in copies:
        copy.start()
    lane = lax.broadcasted_iota(jnp.int32, (2 * slots, LANES), 1).astype(MASK)
    zeros = jnp.zeros((2 * slots, LANES), jnp.bfloat16)
    for step in range(pitch):
        pairs_ref[blocks * pitch + step] = zeros
    for turn in range(2):
        rows_ref[turn, chunks * slots :] = jnp.zeros((slots, LANES), jnp.float32)
    for copy in copies:
        copy.wait()
    fetch.wait()

    def place(owner, carry):
        held = [at_ref[pieces + owner * 2 + half] for half in range(2)]
        for within in range(per_off):
            block = owner * per_off + within
            turn = within % 2
            for slot in range(slots):
                source = codes_ref[held[slot // 4], (slot % 4) * per_off + within] * 2 + slot // 4
                rows_ref[turn, pl.ds(slot, chunks, stride=slots), :] = traces_ref[source, block].astype(jnp.float32)
            start = block * pitch
            for step in range(pitch):
                near = rows_ref[turn, step * slots : (step + 1) * slots]
                far = rows_ref[turn, (step + halves) * slots : (step + halves + 1) * slots]
                pairs_ref[start + step] = jnp.concatenate([near, far], axis=0).astype(jnp.bfloat16)
        return carry

    lax.fori_loop(0, blocks // per_off, place, 0)

    def one_tile(tile, carry):
        count = 0
        for block in range(blocks):
            row = ((block // per_off) * tiles + tile) * LANES
            within = block % per_off
            list_ref[count] = row + within * groups
            count = count + meta_ref[row + per_off * groups + within]
        for more in range(TURNS - 1):
            list_ref[count + more] = per_off * groups + per_off

        def add(step, sums):
            sums = list(sums)
            for turn in range(TURNS):
                entry = list_ref[TURNS * step + turn]
                for group in range(groups):
                    code = meta_ref[entry + group]
                    base = code >> CODE_SHIFT
                    back = code & (LANES - 1)
                    mask = lane >= ((-jnp.broadcast_to(code, (2 * slots, LANES))) & (LANES - 1)).astype(MASK)
                    piece = [pairs_ref[base + step_] for step_ in range(halves + 1)]
                    for part in range(halves):
                        mixed = jnp.where(mask, piece[part], piece[part + 1])
                        turned = pltpu.roll(mixed, back, 1).astype(jnp.float32)
                        for side in range(2):
                            sums[group * parts + side * halves + part] += turned[side * slots : (side + 1) * slots]
            return tuple(sums)

        zero = tuple(jnp.zeros((slots, LANES), jnp.float32) for _ in range(groups * parts))
        sums = lax.fori_loop(0, (count + TURNS - 1) // TURNS, add, zero)
        for group in range(groups):
            for part in range(parts):
                sums_ref[tile, group, :, part * LANES : (part + 1) * LANES] = sums[group * parts + part].astype(jnp.bfloat16)
        pltpu.make_async_copy(sums_ref.at[tile], out_ref.at[tile], out_sems.at[tile]).start()
        return carry

    lax.fori_loop(0, tiles, one_tile, 0)
    for tile in range(tiles):
        pltpu.make_async_copy(sums_ref.at[tile], out_ref.at[tile], out_sems.at[tile]).wait()


def image_kernel(off_ref, stacked_ref, interp_ref, amp_ref, *refs, scale):
    *out_refs, image_ref = refs
    sources, groups, slots, window = stacked_ref.shape
    rows, pixels = out_refs[0].shape
    pixels = pixels // groups
    for group in range(groups):
        stacked = stacked_ref[:, group].reshape(sources * slots, window)
        depth = lax.dot_general(interp_ref[group], stacked, (((1,), (1,)), ((), ())), preferred_element_type=jnp.float32)
        high = depth.astype(jnp.bfloat16)
        low = (depth - high.astype(jnp.float32)).astype(jnp.bfloat16)
        amp = amp_ref[group]
        image = jnp.dot(high, amp, preferred_element_type=jnp.float32) + jnp.dot(low, amp, preferred_element_type=jnp.float32)
        image_ref[:, group * pixels : (group + 1) * pixels] = image * scale
    for apart, ref in enumerate(out_refs):
        ref[...] = image_ref[pl.ds(pl.multiple_of((off_ref[0] ^ apart) * rows, rows), rows), :].astype(ref.dtype)


def join_kernel(off_ref, *refs):
    out_ref = refs[-1]
    for apart, ref in enumerate(refs[:-1]):
        width = ref.shape[1]
        start = pl.multiple_of((off_ref[0] ^ apart) * width, LANES)
        out_ref[:, pl.ds(start, width)] = ref[...].astype(out_ref.dtype)


def ring_pairs(step):
    return [(z, (z + step) % 4) for z in range(4)]


def local(shot_traces, assign, aperture, band, interp, amp):
    blocks, samples = shot_traces.shape[1], shot_traces.shape[3]
    per_off, all_groups = band.shape
    offs = blocks // per_off
    groups = all_groups // offs
    tiles = lax.axis_size("x") * lax.axis_size("y")
    window, depth = interp.shape[1], interp.shape[2]
    pixels = amp.shape[2]
    chunks = samples // LANES
    zh, core, zl = lax.axis_index("zh"), lax.axis_index("core"), lax.axis_index("zl")
    z = zh * 2 + zl
    off = zh * 2 + core
    swap = [(0, 1), (1, 0)]

    smem = pl.BlockSpec(memory_space=pltpu.SMEM)
    vmem = pl.BlockSpec(memory_space=pltpu.VMEM)
    anywhere = pl.BlockSpec(memory_space=pl.ANY)

    pitch = chunks - window // LANES // 2 + 1
    sent, row = pl.pallas_call(
        functools.partial(prepare_kernel, offs=offs, pitch=pitch),
        out_shape=[
            pltpu.VMEM((blocks + 1, chunks, LANES), jnp.bfloat16),
            pltpu.VMEM((offs * tiles, LANES), jnp.int32),
        ],
        in_specs=[smem, smem, smem, smem, vmem],
        out_specs=[vmem, vmem],
        scratch_shapes=[pltpu.VMEM((blocks * chunks, LANES), jnp.float32)],
        name="prepare_traces",
    )(off.reshape(1), jnp.transpose(assign[:, 0, :]), band, jnp.transpose(aperture), shot_traces[0, :, 0, :])
    steps = (1, 3, 2)
    ring = [lax.ppermute(sent, ("zh", "zl"), ring_pairs(step)) for step in steps]

    meta = lax.all_to_all(row, OFF + PLANE, 0, 0, tiled=True)

    *ring, meta = lax.optimization_barrier((*ring, meta))
    column = [sent, *ring]
    pieces = column + [lax.ppermute(piece, "core", swap) for piece in column]
    at = [None] * len(pieces)
    where = [0] * len(pieces)
    for turn in range(2):
        for index, step in enumerate((0,) + steps):
            from_z = (z - step) % 4
            spot = (from_z // 2) * 4 + (core ^ turn) * 2 + from_z % 2
            at[turn * 4 + index] = spot
            for want in range(len(pieces)):
                where[want] = where[want] + jnp.where(spot == want, turn * 4 + index, 0)
    at = jnp.stack(at + where).astype(jnp.int32)

    stacked = pl.pallas_call(
        functools.partial(
            stack_kernel, pieces=len(pieces), blocks=blocks, chunks=chunks, per_off=per_off, tiles=tiles, groups=groups, window=window
        ),
        out_shape=jax.ShapeDtypeStruct((tiles, groups, SUB, window), jnp.bfloat16),
        in_specs=[smem, smem] + [vmem] * len(pieces),
        out_specs=anywhere,
        scratch_shapes=[
            pltpu.VMEM((tiles, groups, SUB, window), jnp.bfloat16),
            pltpu.VMEM((len(pieces), blocks + 1, chunks, LANES), jnp.bfloat16),
            pltpu.VMEM((2, (chunks + 1) * SUB, LANES), jnp.float32),
            pltpu.VMEM(((blocks + 1) * pitch, 2 * SUB, LANES), jnp.bfloat16),
            pltpu.VMEM((len(pieces), LANES), jnp.int32),
            pltpu.SMEM((len(pieces), LANES), jnp.int32),
            pltpu.SMEM((blocks + TURNS - 1,), jnp.int32),
            pltpu.SemaphoreType.DMA((len(pieces) + 1,)),
            pltpu.SemaphoreType.DMA((tiles,)),
        ],
        name="stack_windows",
    )(at, meta.reshape(-1), *map(in_vmem, pieces))

    arrived = lax.all_to_all(stacked, PLANE, 0, 0, tiled=True)

    interp_here = lax.dynamic_slice_in_dim(jnp.swapaxes(interp, 1, 2), off * groups, groups, 0)
    amp_here = lax.dynamic_slice_in_dim(amp, off * groups, groups, 0)
    strip = (depth // offs, groups * pixels)
    own, beside, far, across = pl.pallas_call(
        functools.partial(image_kernel, scale=1.0 / math.sqrt(blocks)),
        out_shape=[pltpu.VMEM(strip, jnp.float32)] + [pltpu.VMEM(strip, jnp.bfloat16)] * 3,
        in_specs=[smem, vmem, vmem, vmem],
        out_specs=[vmem] * 4,
        scratch_shapes=[pltpu.VMEM((depth, groups * pixels), jnp.float32)],
        name="image_groups",
    )(off.reshape(1), in_vmem(arrived), in_vmem(interp_here), in_vmem(amp_here))

    beside = lax.ppermute(beside, "core", swap)
    far = lax.ppermute(far, "zh", swap)
    across = lax.ppermute(across, OFF, [(index, index ^ 3) for index in range(offs)])
    return pl.pallas_call(
        join_kernel,
        out_shape=jax.ShapeDtypeStruct((depth // offs, offs * groups * pixels), jnp.float32),
        in_specs=[smem] + [vmem] * 4,
        out_specs=vmem,
        name="join_groups",
    )(off.reshape(1), *map(in_vmem, (own, beside, far, across)))


def solution(mesh):
    fine = Mesh(mesh.devices.reshape(2, 2, 4, 4, 2), EVERY)
    placed = (
        P(OFF, None, IMG, None),
        P(OFF, IMG, None),
        P(OFF, IMG),
        P(OFF, IMG),
        P(IMG, None, None),
        P(IMG, None, None),
    )
    return jax.shard_map(local, mesh=fine, in_specs=placed, out_specs=P(OFF, IMG), check_vma=False)
```

```python
import functools
import math

import jax
import jax.numpy as jnp
from jax import lax
from jax.experimental import pallas as pl
from jax.experimental.pallas import tpu as pltpu
from jax.sharding import Mesh, PartitionSpec as P

LANES = 128
SUB = 8
OFF = ("zh", "core")
PLANE = ("x", "y")
IMG = ("x", "y", "zl")
EVERY = OFF + IMG
CODE_SHIFT = 7
TURNS = (16, 8)
MASK = jnp.int16


def in_vmem(array):
    return pltpu.with_memory_space_constraint(array, pltpu.VMEM)


def code_rows(off_ref, band_ref, aperture_ref, meta_ref, *, offs, owned, pitch):
    groups = band_ref.shape[1] // offs
    spot = lax.broadcasted_iota(jnp.int32, (SUB, LANES), 1)
    line = lax.broadcasted_iota(jnp.int32, (SUB, LANES), 0)
    here = (off_ref[0] * owned + (spot // groups)) * pitch
    flags = jnp.full((SUB, LANES), (offs * owned * pitch) << CODE_SHIFT, jnp.int32)
    for within in range(owned):
        flags = jnp.where(spot == owned * groups + within, aperture_ref[0, within], flags)
    first = jnp.zeros((SUB, LANES), jnp.int32)
    for within in range(owned):
        for group in range(groups):
            values = jnp.zeros((SUB, LANES), jnp.int32)
            for owner in range(offs):
                values = jnp.where(line == owner, band_ref[within, owner * groups + group], values)
            first = jnp.where(spot == within * groups + group, values, first)
    code = ((here + (first >> 7)) << CODE_SHIFT) | ((-first) & (LANES - 1))
    block = jnp.where(spot < owned * groups, code, flags)
    tiles = meta_ref.shape[0] // offs
    for owner in range(offs):
        row = jnp.broadcast_to(block[owner : owner + 1], (SUB, LANES))
        for tile in range(0, tiles, SUB):
            meta_ref[owner * tiles + tile : owner * tiles + tile + SUB] = row


def prepare_kernel(off_ref, assign_ref, band_ref, aperture_ref, raw_ref, out_ref, sent_ref, rows_ref, traces_ref, meta_ref, sems, *, offs, pitch):
    fetch = pltpu.make_async_copy(raw_ref, traces_ref, sems.at[0])
    fetch.start()
    code_rows(off_ref, band_ref, aperture_ref, meta_ref, offs=offs, owned=assign_ref.shape[1], pitch=pitch)
    send = pltpu.make_async_copy(meta_ref, sent_ref, sems.at[1])
    send.start()
    fetch.wait()
    blocks, samples = traces_ref.shape
    chunks = samples // LANES
    lane = lax.broadcasted_iota(jnp.int32, (blocks, LANES), 1)
    before = jnp.zeros((blocks, LANES), jnp.float32)
    for chunk in range(chunks):
        here = traces_ref[:, chunk * LANES : (chunk + 1) * LANES].astype(jnp.float32)
        turned = pltpu.roll(here, 1, 1)
        rows_ref[pl.ds(chunk, blocks, stride=chunks), :] = here - 0.9 * jnp.where(lane == 0, before, turned)
        before = turned
    for block in range(blocks):
        out_ref[block] = rows_ref[block * chunks : (block + 1) * chunks].astype(out_ref.dtype)
    slots, owned = assign_ref.shape
    spot = lax.broadcasted_iota(jnp.int32, (chunks, LANES), 1)
    codes = jnp.zeros((chunks, LANES), jnp.float32)
    for slot in range(slots):
        for within in range(owned):
            codes = jnp.where(spot == slot * owned + within, assign_ref[slot, within].astype(jnp.float32), codes)
    out_ref[blocks] = codes.astype(out_ref.dtype)
    send.wait()


def spot_of(piece, z, core):
    from_z = (z - ((piece % 4) ^ (piece % 4 >> 1))) & 3
    return (from_z >> 1) * 4 + (core ^ (piece // 4)) * 2 + (from_z & 1)


def stack_kernel(z_ref, core_ref, table_ref, *refs, pieces, blocks, chunks, per_off, tiles, groups, window):
    piece_refs = refs[:pieces]
    out_ref, sums_ref, traces_ref, rows_ref, pairs_ref, words_ref, codes_ref, meta_ref, list_ref, sems, out_sems = refs[pieces:]
    table = pltpu.make_async_copy(table_ref, meta_ref, sems.at[pieces + 1])
    table.start()
    slots = SUB
    parts = window // LANES
    halves = parts // 2
    pitch = chunks - halves + 1
    z, core = z_ref[0], core_ref[0]
    for piece in range(pieces):
        words_ref[piece : piece + 1] = piece_refs[piece][blocks, 0:1, :].astype(jnp.float32).astype(jnp.int32)
    fetch = pltpu.make_async_copy(words_ref, codes_ref, sems.at[pieces])
    fetch.start()
    copies = [
        pltpu.make_async_copy(piece_refs[piece], traces_ref.at[spot_of(piece, z, core)], sems.at[piece])
        for piece in range(pieces)
    ]
    for copy in copies:
        copy.start()
    lane = lax.broadcasted_iota(jnp.int32, (2 * slots, LANES), 1).astype(MASK)
    zeros = jnp.zeros((2 * slots, LANES), jnp.bfloat16)
    for step in range(pitch):
        pairs_ref[blocks * pitch + step] = zeros
    for turn in range(2):
        rows_ref[turn, chunks * slots :] = jnp.zeros((slots, LANES), jnp.float32)
    for copy in copies:
        copy.wait()
    fetch.wait()

    def place(owner, carry):
        steps = [(z - (owner >> 1) * 2 - half) & 3 for half in range(2)]
        held = [(core ^ (owner & 1)) * 4 + (step ^ (step >> 1)) for step in steps]
        for within in range(per_off):
            block = owner * per_off + within
            turn = within % 2
            for slot in range(slots):
                source = codes_ref[held[slot // 4], (slot % 4) * per_off + within] * 2 + slot // 4
                rows_ref[turn, pl.ds(slot, chunks, stride=slots), :] = traces_ref[source, block].astype(jnp.float32)
            start = block * pitch
            for step in range(pitch):
                near = rows_ref[turn, step * slots : (step + 1) * slots]
                far = rows_ref[turn, (step + halves) * slots : (step + halves + 1) * slots]
                pairs_ref[start + step] = jnp.concatenate([near, far], axis=0).astype(jnp.bfloat16)
        return carry

    lax.fori_loop(0, blocks // per_off, place, 0)
    table.wait()

    def one_tile(tile, carry):
        count = 0
        for block in range(blocks):
            row = ((block // per_off) * tiles + tile) * LANES
            within = block % per_off
            list_ref[count] = row + within * groups
            count = count + meta_ref[row + per_off * groups + within]
        for more in range(TURNS[-1] - 1):
            list_ref[count + more] = per_off * groups + per_off

        def add(step, sums, done, turns):
            sums = list(sums)
            for turn in range(turns):
                entry = list_ref[done + turns * step + turn]
                for group in range(groups):
                    code = meta_ref[entry + group]
                    base = code >> CODE_SHIFT
                    back = code & (LANES - 1)
                    mask = lane >= ((-jnp.broadcast_to(code, (2 * slots, LANES))) & (LANES - 1)).astype(MASK)
                    piece = [pairs_ref[base + step_] for step_ in range(halves + 1)]
                    for part in range(halves):
                        mixed = jnp.where(mask, piece[part], piece[part + 1])
                        turned = pltpu.roll(mixed, back, 1).astype(jnp.float32)
                        for side in range(2):
                            sums[group * parts + side * halves + part] += turned[side * slots : (side + 1) * slots]
            return tuple(sums)

        zero = tuple(jnp.zeros((slots, LANES), jnp.float32) for _ in range(groups * parts))
        sums, done = zero, 0
        for turns in TURNS[:-1]:
            steps = (count - done) // turns
            sums = lax.fori_loop(0, steps, functools.partial(add, done=done, turns=turns), sums)
            done = done + steps * turns
        turns = TURNS[-1]
        sums = lax.fori_loop(0, (count - done + turns - 1) // turns, functools.partial(add, done=done, turns=turns), sums)
        for group in range(groups):
            for part in range(parts):
                sums_ref[tile, group, :, part * LANES : (part + 1) * LANES] = sums[group * parts + part].astype(jnp.bfloat16)
        pltpu.make_async_copy(sums_ref.at[tile], out_ref.at[tile], out_sems.at[tile]).start()
        return carry

    lax.fori_loop(0, tiles, one_tile, 0)
    for tile in range(tiles):
        pltpu.make_async_copy(sums_ref.at[tile], out_ref.at[tile], out_sems.at[tile]).wait()


def image_kernel(off_ref, stacked_ref, interp_ref, amp_ref, *refs, scale):
    *out_refs, image_ref = refs
    sources, groups, slots, window = stacked_ref.shape
    rows, pixels = out_refs[0].shape
    pixels = pixels // groups
    for group in range(groups):
        stacked = stacked_ref[:, group].reshape(sources * slots, window)
        depth = lax.dot_general(interp_ref[group], stacked, (((1,), (1,)), ((), ())), preferred_element_type=jnp.float32)
        high = depth.astype(jnp.bfloat16)
        low = (depth - high.astype(jnp.float32)).astype(jnp.bfloat16)
        amp = amp_ref[group]
        image = jnp.dot(high, amp, preferred_element_type=jnp.float32) + jnp.dot(low, amp, preferred_element_type=jnp.float32)
        image_ref[:, group * pixels : (group + 1) * pixels] = image * scale
    for apart, ref in enumerate(out_refs):
        ref[...] = image_ref[pl.ds(pl.multiple_of((off_ref[0] ^ apart) * rows, rows), rows), :].astype(ref.dtype)


def join_kernel(off_ref, *refs):
    out_ref = refs[-1]
    for apart, ref in enumerate(refs[:-1]):
        width = ref.shape[1]
        start = pl.multiple_of((off_ref[0] ^ apart) * width, LANES)
        out_ref[:, pl.ds(start, width)] = ref[...].astype(out_ref.dtype)


def ring_pairs(step):
    return [(z, (z + step) % 4) for z in range(4)]


def local(shot_traces, assign, aperture, band, interp, amp):
    blocks, samples = shot_traces.shape[1], shot_traces.shape[3]
    per_off, all_groups = band.shape
    offs = blocks // per_off
    groups = all_groups // offs
    tiles = lax.axis_size("x") * lax.axis_size("y")
    window, depth = interp.shape[1], interp.shape[2]
    pixels = amp.shape[2]
    chunks = samples // LANES
    zh, core, zl = lax.axis_index("zh"), lax.axis_index("core"), lax.axis_index("zl")
    z = zh * 2 + zl
    off = zh * 2 + core
    swap = [(0, 1), (1, 0)]

    smem = pl.BlockSpec(memory_space=pltpu.SMEM)
    vmem = pl.BlockSpec(memory_space=pltpu.VMEM)
    anywhere = pl.BlockSpec(memory_space=pl.ANY)

    pitch = chunks - window // LANES // 2 + 1
    sent, row = pl.pallas_call(
        functools.partial(prepare_kernel, offs=offs, pitch=pitch),
        out_shape=[
            pltpu.VMEM((blocks + 1, chunks, LANES), jnp.bfloat16),
            jax.ShapeDtypeStruct((offs * tiles, LANES), jnp.int32),
        ],
        in_specs=[smem, smem, smem, smem, anywhere],
        out_specs=[vmem, anywhere],
        scratch_shapes=[
            pltpu.VMEM((blocks * chunks, LANES), jnp.float32),
            pltpu.VMEM((blocks, samples), jnp.bfloat16),
            pltpu.VMEM((offs * tiles, LANES), jnp.int32),
            pltpu.SemaphoreType.DMA((2,)),
        ],
        name="prepare_traces",
    )(off.reshape(1), jnp.transpose(assign[:, 0, :]), band, jnp.transpose(aperture), shot_traces[0, :, 0, :])
    steps = (1, 3, 2)
    ring = [lax.ppermute(sent, ("zh", "zl"), ring_pairs(step)) for step in steps]

    meta = lax.all_to_all(row, OFF + PLANE, 0, 0, tiled=True)

    *ring, meta = lax.optimization_barrier((*ring, meta))
    column = [sent, *ring]
    pieces = column + [lax.ppermute(piece, "core", swap) for piece in column]
    stacked = pl.pallas_call(
        functools.partial(
            stack_kernel, pieces=len(pieces), blocks=blocks, chunks=chunks, per_off=per_off, tiles=tiles, groups=groups, window=window
        ),
        out_shape=jax.ShapeDtypeStruct((tiles, groups, SUB, window), jnp.bfloat16),
        in_specs=[smem, smem, anywhere] + [vmem] * len(pieces),
        out_specs=anywhere,
        scratch_shapes=[
            pltpu.VMEM((tiles, groups, SUB, window), jnp.bfloat16),
            pltpu.VMEM((len(pieces), blocks + 1, chunks, LANES), jnp.bfloat16),
            pltpu.VMEM((2, (chunks + 1) * SUB, LANES), jnp.float32),
            pltpu.VMEM(((blocks + 1) * pitch, 2 * SUB, LANES), jnp.bfloat16),
            pltpu.VMEM((len(pieces), LANES), jnp.int32),
            pltpu.SMEM((len(pieces), LANES), jnp.int32),
            pltpu.SMEM((offs * tiles * LANES,), jnp.int32),
            pltpu.SMEM((blocks + TURNS[-1] - 1,), jnp.int32),
            pltpu.SemaphoreType.DMA((len(pieces) + 2,)),
            pltpu.SemaphoreType.DMA((tiles,)),
        ],
        name="stack_windows",
    )(z.reshape(1), core.reshape(1), in_vmem(meta.reshape(-1)), *map(in_vmem, pieces))

    arrived = lax.all_to_all(stacked, PLANE, 0, 0, tiled=True)

    interp_here = lax.dynamic_slice_in_dim(jnp.swapaxes(interp, 1, 2), off * groups, groups, 0)
    amp_here = lax.dynamic_slice_in_dim(amp, off * groups, groups, 0)
    strip = (depth // offs, groups * pixels)
    own, beside, far, across = pl.pallas_call(
        functools.partial(image_kernel, scale=1.0 / math.sqrt(blocks)),
        out_shape=[pltpu.VMEM(strip, jnp.float32)] + [pltpu.VMEM(strip, jnp.bfloat16)] * 3,
        in_specs=[smem, vmem, vmem, vmem],
        out_specs=[vmem] * 4,
        scratch_shapes=[pltpu.VMEM((depth, groups * pixels), jnp.float32)],
        name="image_groups",
    )(off.reshape(1), in_vmem(arrived), in_vmem(interp_here), in_vmem(amp_here))

    beside = lax.ppermute(beside, "core", swap)
    far = lax.ppermute(far, "zh", swap)
    across = lax.ppermute(across, OFF, [(index, index ^ 3) for index in range(offs)])
    return pl.pallas_call(
        join_kernel,
        out_shape=jax.ShapeDtypeStruct((depth // offs, offs * groups * pixels), jnp.float32),
        in_specs=[smem] + [vmem] * 4,
        out_specs=vmem,
        name="join_groups",
    )(off.reshape(1), *map(in_vmem, (own, beside, far, across)))


def solution(mesh):
    fine = Mesh(mesh.devices.reshape(2, 2, 4, 4, 2), EVERY)
    placed = (
        P(OFF, None, IMG, None),
        P(OFF, IMG, None),
        P(OFF, IMG),
        P(OFF, IMG),
        P(IMG, None, None),
        P(IMG, None, None),
    )
    return jax.shard_map(local, mesh=fine, in_specs=placed, out_specs=P(OFF, IMG), check_vma=False)
```

```python
import functools
import math

import jax
import jax.numpy as jnp
from jax import lax
from jax.experimental import pallas as pl
from jax.experimental.pallas import tpu as pltpu
from jax.sharding import Mesh, PartitionSpec as P

LANES = 128
SUB = 8
OFF = ("zh", "core")
PLANE = ("x", "y")
IMG = ("x", "y", "zl")
EVERY = OFF + IMG
CODE_SHIFT = 7
TURNS = (16, 8)
MASK = jnp.int16


def in_vmem(array):
    return pltpu.with_memory_space_constraint(array, pltpu.VMEM)


def code_rows(off_ref, band_ref, aperture_ref, meta_ref, *, offs, owned, pitch):
    groups = band_ref.shape[1] // offs
    spot = lax.broadcasted_iota(jnp.int32, (SUB, LANES), 1)
    line = lax.broadcasted_iota(jnp.int32, (SUB, LANES), 0)
    here = jnp.zeros((SUB, LANES), jnp.int32)
    first = jnp.zeros((SUB, LANES), jnp.int32)
    count = 0
    for within in range(owned):
        inside = aperture_ref[0, within]
        turn = owned + inside * (count - owned)
        count = count + inside
        here = jnp.where(spot // groups == turn, (off_ref[0] * owned + within) * pitch, here)
        for group in range(groups):
            values = jnp.zeros((SUB, LANES), jnp.int32)
            for owner in range(offs):
                values = jnp.where(line == owner, band_ref[within, owner * groups + group], values)
            first = jnp.where(spot == turn * groups + group, values, first)
    flags = jnp.where(spot == owned * groups, count, (offs * owned * pitch) << CODE_SHIFT)
    code = ((here + (first >> 7)) << CODE_SHIFT) | ((-first) & (LANES - 1))
    block = jnp.where(spot < owned * groups, code, flags)
    tiles = meta_ref.shape[0] // offs
    for owner in range(offs):
        row = jnp.broadcast_to(block[owner : owner + 1], (SUB, LANES))
        for tile in range(0, tiles, SUB):
            meta_ref[owner * tiles + tile : owner * tiles + tile + SUB] = row


def prepare_kernel(off_ref, *refs, offs, pitch):
    *sources, out_ref, sent_ref, rows_ref, traces_ref, assign_ref, band_ref, aperture_ref, meta_ref, sems = refs
    fetch, *smalls = [
        pltpu.make_async_copy(source, held, sems.at[index])
        for index, (source, held) in enumerate(zip(sources, (traces_ref, assign_ref, band_ref, aperture_ref)))
    ]
    for copy in (fetch, *smalls):
        copy.start()
    for copy in smalls:
        copy.wait()
    code_rows(off_ref, band_ref, aperture_ref, meta_ref, offs=offs, owned=assign_ref.shape[1], pitch=pitch)
    send = pltpu.make_async_copy(meta_ref, sent_ref, sems.at[4])
    send.start()
    fetch.wait()
    blocks, samples = traces_ref.shape
    chunks = samples // LANES
    lane = lax.broadcasted_iota(jnp.int32, (blocks, LANES), 1)
    before = jnp.zeros((blocks, LANES), jnp.float32)
    for chunk in range(chunks):
        here = traces_ref[:, chunk * LANES : (chunk + 1) * LANES].astype(jnp.float32)
        turned = pltpu.roll(here, 1, 1)
        rows_ref[pl.ds(chunk, blocks, stride=chunks), :] = here - 0.9 * jnp.where(lane == 0, before, turned)
        before = turned
    for block in range(blocks):
        out_ref[block] = rows_ref[block * chunks : (block + 1) * chunks].astype(out_ref.dtype)
    slots, owned = assign_ref.shape
    spot = lax.broadcasted_iota(jnp.int32, (chunks, LANES), 1)
    codes = jnp.zeros((chunks, LANES), jnp.float32)
    for slot in range(slots):
        for within in range(owned):
            codes = jnp.where(spot == slot * owned + within, assign_ref[slot, within].astype(jnp.float32), codes)
    out_ref[blocks] = codes.astype(out_ref.dtype)
    send.wait()


def spot_of(piece, z, core):
    from_z = (z - ((piece % 4) ^ (piece % 4 >> 1))) & 3
    return (from_z >> 1) * 4 + (core ^ (piece // 4)) * 2 + (from_z & 1)


def stack_kernel(z_ref, core_ref, table_ref, *refs, pieces, blocks, chunks, per_off, tiles, groups, window):
    piece_refs = refs[:pieces]
    out_ref, sums_ref, traces_ref, rows_ref, pairs_ref, words_ref, codes_ref, meta_ref, list_ref, sems, out_sems = refs[pieces:]
    table = pltpu.make_async_copy(table_ref, meta_ref, sems.at[pieces + 1])
    table.start()
    slots = SUB
    parts = window // LANES
    halves = parts // 2
    pitch = chunks - halves + 1
    z, core = z_ref[0], core_ref[0]
    for piece in range(pieces):
        words_ref[piece : piece + 1] = piece_refs[piece][blocks, 0:1, :].astype(jnp.float32).astype(jnp.int32)
    fetch = pltpu.make_async_copy(words_ref, codes_ref, sems.at[pieces])
    fetch.start()
    copies = [
        pltpu.make_async_copy(piece_refs[piece], traces_ref.at[spot_of(piece, z, core)], sems.at[piece])
        for piece in range(pieces)
    ]
    for copy in copies:
        copy.start()
    lane = lax.broadcasted_iota(jnp.int32, (2 * slots, LANES), 1).astype(MASK)
    zeros = jnp.zeros((2 * slots, LANES), jnp.bfloat16)
    for step in range(pitch):
        pairs_ref[blocks * pitch + step] = zeros
    for turn in range(2):
        rows_ref[turn, chunks * slots :] = jnp.zeros((slots, LANES), jnp.float32)
    for copy in copies:
        copy.wait()
    fetch.wait()

    def place(owner, carry):
        steps = [(z - (owner >> 1) * 2 - half) & 3 for half in range(2)]
        held = [(core ^ (owner & 1)) * 4 + (step ^ (step >> 1)) for step in steps]
        for within in range(per_off):
            block = owner * per_off + within
            turn = within % 2
            for slot in range(slots):
                source = codes_ref[held[slot // 4], (slot % 4) * per_off + within] * 2 + slot // 4
                rows_ref[turn, pl.ds(slot, chunks, stride=slots), :] = traces_ref[source, block].astype(jnp.float32)
            start = block * pitch
            for step in range(pitch):
                near = rows_ref[turn, step * slots : (step + 1) * slots]
                far = rows_ref[turn, (step + halves) * slots : (step + halves + 1) * slots]
                pairs_ref[start + step] = jnp.concatenate([near, far], axis=0).astype(jnp.bfloat16)
        return carry

    lax.fori_loop(0, blocks // per_off, place, 0)
    table.wait()

    def one_tile(tile, carry):
        count = 0
        for owner in range(blocks // per_off):
            row = (owner * tiles + tile) * LANES
            for turn in range(per_off):
                list_ref[count + turn] = row + turn * groups
            count = count + meta_ref[row + per_off * groups]
        for more in range(TURNS[-1] - 1):
            list_ref[count + more] = per_off * groups + per_off

        def add(step, sums, done, turns):
            sums = list(sums)
            for turn in range(turns):
                entry = list_ref[done + turns * step + turn]
                for group in range(groups):
                    code = meta_ref[entry + group]
                    base = code >> CODE_SHIFT
                    back = code & (LANES - 1)
                    mask = lane >= ((-jnp.broadcast_to(code, (2 * slots, LANES))) & (LANES - 1)).astype(MASK)
                    piece = [pairs_ref[base + step_] for step_ in range(halves + 1)]
                    for part in range(halves):
                        mixed = jnp.where(mask, piece[part], piece[part + 1])
                        turned = pltpu.roll(mixed, back, 1).astype(jnp.float32)
                        for side in range(2):
                            sums[group * parts + side * halves + part] += turned[side * slots : (side + 1) * slots]
            return tuple(sums)

        zero = tuple(jnp.zeros((slots, LANES), jnp.float32) for _ in range(groups * parts))
        sums, done = zero, 0
        for turns in TURNS[:-1]:
            steps = (count - done) // turns
            sums = lax.fori_loop(0, steps, functools.partial(add, done=done, turns=turns), sums)
            done = done + steps * turns
        turns = TURNS[-1]
        sums = lax.fori_loop(0, (count - done + turns - 1) // turns, functools.partial(add, done=done, turns=turns), sums)
        for group in range(groups):
            for part in range(parts):
                sums_ref[tile, group, :, part * LANES : (part + 1) * LANES] = sums[group * parts + part].astype(jnp.bfloat16)
        pltpu.make_async_copy(sums_ref.at[tile], out_ref.at[tile], out_sems.at[tile]).start()
        return carry

    lax.fori_loop(0, tiles, one_tile, 0)
    for tile in range(tiles):
        pltpu.make_async_copy(sums_ref.at[tile], out_ref.at[tile], out_sems.at[tile]).wait()


def image_kernel(off_ref, stacked_ref, interp_ref, amp_ref, *refs, scale):
    *out_refs, image_ref = refs
    sources, groups, slots, window = stacked_ref.shape
    rows, pixels = out_refs[0].shape
    pixels = pixels // groups
    for group in range(groups):
        stacked = stacked_ref[:, group].reshape(sources * slots, window)
        depth = lax.dot_general(interp_ref[group], stacked, (((1,), (1,)), ((), ())), preferred_element_type=jnp.float32)
        high = depth.astype(jnp.bfloat16)
        low = (depth - high.astype(jnp.float32)).astype(jnp.bfloat16)
        amp = amp_ref[group]
        image = jnp.dot(high, amp, preferred_element_type=jnp.float32) + jnp.dot(low, amp, preferred_element_type=jnp.float32)
        image_ref[:, group * pixels : (group + 1) * pixels] = image * scale
    for apart, ref in enumerate(out_refs):
        ref[...] = image_ref[pl.ds(pl.multiple_of((off_ref[0] ^ apart) * rows, rows), rows), :].astype(ref.dtype)


def join_kernel(off_ref, *refs):
    out_ref = refs[-1]
    for apart, ref in enumerate(refs[:-1]):
        width = ref.shape[1]
        start = pl.multiple_of((off_ref[0] ^ apart) * width, LANES)
        out_ref[:, pl.ds(start, width)] = ref[...].astype(out_ref.dtype)


def ring_pairs(step):
    return [(z, (z + step) % 4) for z in range(4)]


def local(shot_traces, assign, aperture, band, interp, amp):
    blocks, samples = shot_traces.shape[1], shot_traces.shape[3]
    per_off, all_groups = band.shape
    offs = blocks // per_off
    groups = all_groups // offs
    tiles = lax.axis_size("x") * lax.axis_size("y")
    window, depth = interp.shape[1], interp.shape[2]
    pixels = amp.shape[2]
    chunks = samples // LANES
    zh, core, zl = lax.axis_index("zh"), lax.axis_index("core"), lax.axis_index("zl")
    z = zh * 2 + zl
    off = zh * 2 + core
    swap = [(0, 1), (1, 0)]

    smem = pl.BlockSpec(memory_space=pltpu.SMEM)
    vmem = pl.BlockSpec(memory_space=pltpu.VMEM)
    anywhere = pl.BlockSpec(memory_space=pl.ANY)

    pitch = chunks - window // LANES // 2 + 1
    sent, row = pl.pallas_call(
        functools.partial(prepare_kernel, offs=offs, pitch=pitch),
        out_shape=[
            pltpu.VMEM((blocks + 1, chunks, LANES), jnp.bfloat16),
            jax.ShapeDtypeStruct((offs * tiles, LANES), jnp.int32),
        ],
        in_specs=[smem] + [anywhere] * 4,
        out_specs=[vmem, anywhere],
        scratch_shapes=[
            pltpu.VMEM((blocks * chunks, LANES), jnp.float32),
            pltpu.VMEM((blocks, samples), jnp.bfloat16),
            pltpu.SMEM((assign.shape[2], per_off), jnp.int32),
            pltpu.SMEM((per_off, all_groups), jnp.int32),
            pltpu.SMEM((1, per_off), jnp.int32),
            pltpu.VMEM((offs * tiles, LANES), jnp.int32),
            pltpu.SemaphoreType.DMA((5,)),
        ],
        name="prepare_traces",
    )(off.reshape(1), shot_traces[0, :, 0, :], jnp.transpose(assign[:, 0, :]), band, jnp.transpose(aperture))
    steps = (1, 3, 2)
    ring = [lax.ppermute(sent, ("zh", "zl"), ring_pairs(step)) for step in steps]

    meta = lax.all_to_all(row, OFF + PLANE, 0, 0, tiled=True)

    *ring, meta = lax.optimization_barrier((*ring, meta))
    column = [sent, *ring]
    pieces = column + [lax.ppermute(piece, "core", swap) for piece in column]
    stacked = pl.pallas_call(
        functools.partial(
            stack_kernel, pieces=len(pieces), blocks=blocks, chunks=chunks, per_off=per_off, tiles=tiles, groups=groups, window=window
        ),
        out_shape=jax.ShapeDtypeStruct((tiles, groups, SUB, window), jnp.bfloat16),
        in_specs=[smem, smem, anywhere] + [vmem] * len(pieces),
        out_specs=anywhere,
        scratch_shapes=[
            pltpu.VMEM((tiles, groups, SUB, window), jnp.bfloat16),
            pltpu.VMEM((len(pieces), blocks + 1, chunks, LANES), jnp.bfloat16),
            pltpu.VMEM((2, (chunks + 1) * SUB, LANES), jnp.float32),
            pltpu.VMEM(((blocks + 1) * pitch, 2 * SUB, LANES), jnp.bfloat16),
            pltpu.VMEM((len(pieces), LANES), jnp.int32),
            pltpu.SMEM((len(pieces), LANES), jnp.int32),
            pltpu.SMEM((offs * tiles * LANES,), jnp.int32),
            pltpu.SMEM((blocks + TURNS[-1] - 1,), jnp.int32),
            pltpu.SemaphoreType.DMA((len(pieces) + 2,)),
            pltpu.SemaphoreType.DMA((tiles,)),
        ],
        name="stack_windows",
    )(z.reshape(1), core.reshape(1), in_vmem(meta.reshape(-1)), *map(in_vmem, pieces))

    arrived = lax.all_to_all(stacked, PLANE, 0, 0, tiled=True)

    interp_here = lax.dynamic_slice_in_dim(jnp.swapaxes(interp, 1, 2), off * groups, groups, 0)
    amp_here = lax.dynamic_slice_in_dim(amp, off * groups, groups, 0)
    strip = (depth // offs, groups * pixels)
    own, beside, far, across = pl.pallas_call(
        functools.partial(image_kernel, scale=1.0 / math.sqrt(blocks)),
        out_shape=[pltpu.VMEM(strip, jnp.float32)] + [pltpu.VMEM(strip, jnp.bfloat16)] * 3,
        in_specs=[smem, vmem, vmem, vmem],
        out_specs=[vmem] * 4,
        scratch_shapes=[pltpu.VMEM((depth, groups * pixels), jnp.float32)],
        name="image_groups",
    )(off.reshape(1), in_vmem(arrived), in_vmem(interp_here), in_vmem(amp_here))

    beside = lax.ppermute(beside, "core", swap)
    far = lax.ppermute(far, "zh", swap)
    across = lax.ppermute(across, OFF, [(index, index ^ 3) for index in range(offs)])
    return pl.pallas_call(
        join_kernel,
        out_shape=jax.ShapeDtypeStruct((depth // offs, offs * groups * pixels), jnp.float32),
        in_specs=[smem] + [vmem] * 4,
        out_specs=vmem,
        name="join_groups",
    )(off.reshape(1), *map(in_vmem, (own, beside, far, across)))


def solution(mesh):
    fine = Mesh(mesh.devices.reshape(2, 2, 4, 4, 2), EVERY)
    placed = (
        P(OFF, None, IMG, None),
        P(OFF, IMG, None),
        P(OFF, IMG),
        P(OFF, IMG),
        P(IMG, None, None),
        P(IMG, None, None),
    )
    return jax.shard_map(local, mesh=fine, in_specs=placed, out_specs=P(OFF, IMG), check_vma=False)
```

```python
import functools
import math

import jax
import jax.numpy as jnp
from jax import lax
from jax.experimental import pallas as pl
from jax.experimental.pallas import tpu as pltpu
from jax.sharding import Mesh, PartitionSpec as P

LANES = 128
SUB = 8
OFF = ("zh", "core")
PLANE = ("x", "y")
IMG = ("x", "y", "zl")
EVERY = OFF + IMG
CODE_SHIFT = 7
TURNS = (16, 8)
MASK = jnp.int16
VMEM_BYTES = 24 * 2**20


def in_hbm(array):
    return pltpu.with_memory_space_constraint(array, pltpu.HBM)


def in_vmem(array):
    return pltpu.with_memory_space_constraint(array, pltpu.VMEM)


def code_rows(off_ref, band_ref, aperture_ref, meta_ref, *, offs, owned, pitch):
    groups = band_ref.shape[1] // offs
    spot = lax.broadcasted_iota(jnp.int32, (SUB, LANES), 1)
    line = lax.broadcasted_iota(jnp.int32, (SUB, LANES), 0)
    here = jnp.zeros((SUB, LANES), jnp.int32)
    first = jnp.zeros((SUB, LANES), jnp.int32)
    count = 0
    for within in range(owned):
        inside = aperture_ref[0, within]
        turn = owned + inside * (count - owned)
        count = count + inside
        here = jnp.where(spot // groups == turn, (off_ref[0] * owned + within) * pitch, here)
        for group in range(groups):
            values = jnp.zeros((SUB, LANES), jnp.int32)
            for owner in range(offs):
                values = jnp.where(line == owner, band_ref[within, owner * groups + group], values)
            first = jnp.where(spot == turn * groups + group, values, first)
    flags = jnp.where(spot == owned * groups, count, (offs * owned * pitch) << CODE_SHIFT)
    code = ((here + (first >> 7)) << CODE_SHIFT) | ((-first) & (LANES - 1))
    block = jnp.where(spot < owned * groups, code, flags)
    tiles = meta_ref.shape[0] // offs
    for core in range(2):
        row = jnp.where(line % 2 == 0, block[core : core + 1], block[2 + core : 3 + core])
        for start in range(0, 2 * tiles, SUB):
            meta_ref[core * 2 * tiles + start : core * 2 * tiles + start + SUB] = row


def prepare_kernel(off_ref, *refs, offs, pitch):
    *sources, out_ref, sent_ref, rows_ref, traces_ref, assign_ref, band_ref, aperture_ref, meta_ref, sems = refs
    fetch, *smalls = [
        pltpu.make_async_copy(source, held, sems.at[index])
        for index, (source, held) in enumerate(zip(sources, (traces_ref, assign_ref, band_ref, aperture_ref)))
    ]
    for copy in (fetch, *smalls):
        copy.start()
    for copy in smalls:
        copy.wait()
    code_rows(off_ref, band_ref, aperture_ref, meta_ref, offs=offs, owned=assign_ref.shape[1], pitch=pitch)
    send = pltpu.make_async_copy(meta_ref, sent_ref, sems.at[4])
    send.start()
    fetch.wait()
    blocks, samples = traces_ref.shape
    chunks = samples // LANES
    lane = lax.broadcasted_iota(jnp.int32, (blocks, LANES), 1)
    before = jnp.zeros((blocks, LANES), jnp.float32)
    for chunk in range(chunks):
        here = traces_ref[:, chunk * LANES : (chunk + 1) * LANES].astype(jnp.float32)
        turned = pltpu.roll(here, 1, 1)
        rows_ref[pl.ds(chunk, blocks, stride=chunks), :] = here - 0.9 * jnp.where(lane == 0, before, turned)
        before = turned
    for block in range(blocks):
        out_ref[block] = rows_ref[block * chunks : (block + 1) * chunks].astype(out_ref.dtype)
    slots, owned = assign_ref.shape
    spot = lax.broadcasted_iota(jnp.int32, (chunks, LANES), 1)
    codes = jnp.zeros((chunks, LANES), jnp.float32)
    for slot in range(slots):
        for within in range(owned):
            codes = jnp.where(spot == slot * owned + within, assign_ref[slot, within].astype(jnp.float32), codes)
    out_ref[blocks] = codes.astype(out_ref.dtype)
    send.wait()


def spot_of(piece, z, core):
    from_z = (z - ((piece % 4) ^ (piece % 4 >> 1))) & 3
    return (from_z >> 1) * 4 + (core ^ (piece // 4)) * 2 + (from_z & 1)


def place_kernel(z_ref, core_ref, *refs, pieces, blocks, chunks, per_off, tiles, groups, window):
    piece_refs = refs[:pieces]
    pairs_ref, traces_ref, rows_ref, words_ref, codes_ref, sems = refs[pieces:]
    slots = SUB
    parts = window // LANES
    halves = parts // 2
    pitch = chunks - halves + 1
    z, core = z_ref[0], core_ref[0]
    for piece in range(pieces):
        words_ref[piece : piece + 1] = piece_refs[piece][blocks, 0:1, :].astype(jnp.float32).astype(jnp.int32)
    fetch = pltpu.make_async_copy(words_ref, codes_ref, sems.at[pieces])
    fetch.start()
    copies = [
        pltpu.make_async_copy(piece_refs[piece], traces_ref.at[spot_of(piece, z, core)], sems.at[piece])
        for piece in range(pieces)
    ]
    for copy in copies:
        copy.start()
    lane = lax.broadcasted_iota(jnp.int32, (2 * slots, LANES), 1).astype(MASK)
    zeros = jnp.zeros((2 * slots, LANES), jnp.bfloat16)
    for step in range(pitch):
        pairs_ref[blocks * pitch + step] = zeros
    for turn in range(2):
        rows_ref[turn, chunks * slots :] = jnp.zeros((slots, LANES), jnp.float32)
    for copy in copies:
        copy.wait()
    fetch.wait()

    def place(owner, carry):
        steps = [(z - (owner >> 1) * 2 - half) & 3 for half in range(2)]
        held = [(core ^ (owner & 1)) * 4 + (step ^ (step >> 1)) for step in steps]
        for within in range(per_off):
            block = owner * per_off + within
            turn = within % 2
            for slot in range(slots):
                source = codes_ref[held[slot // 4], (slot % 4) * per_off + within] * 2 + slot // 4
                rows_ref[turn, pl.ds(slot, chunks, stride=slots), :] = traces_ref[source, block].astype(jnp.float32)
            start = block * pitch
            for step in range(pitch):
                near = rows_ref[turn, step * slots : (step + 1) * slots]
                far = rows_ref[turn, (step + halves) * slots : (step + halves + 1) * slots]
                pairs_ref[start + step] = jnp.concatenate([near, far], axis=0).astype(jnp.bfloat16)
        return carry

    lax.fori_loop(0, blocks // per_off, place, 0)


def stack_kernel(z_ref, near_ref, far_ref, pairs_ref, out_ref, sums_ref, meta_ref, list_ref, sems, out_sems, *, blocks, chunks, per_off, tiles, groups, window):
    z = z_ref[0]
    span = near_ref.shape[0]
    fetches = [
        pltpu.make_async_copy(ref, meta_ref.at[pl.ds(index * span, span)], sems.at[index])
        for index, ref in enumerate((near_ref, far_ref))
    ]
    for table in fetches:
        table.start()
    slots = SUB
    parts = window // LANES
    halves = parts // 2
    pitch = chunks - halves + 1
    lane = lax.broadcasted_iota(jnp.int32, (2 * slots, LANES), 1).astype(MASK)
    for table in fetches:
        table.wait()

    def one_tile(tile, carry):
        count = 0
        for owner in range(blocks // per_off):
            row = owner // 2 * span + ((owner % 2 * tiles + tile) * 2 + (z >> 1)) * LANES
            for turn in range(per_off):
                list_ref[count + turn] = row + turn * groups
            count = count + meta_ref[row + per_off * groups]
        for more in range(TURNS[-1] - 1):
            list_ref[count + more] = per_off * groups + per_off

        def add(step, sums, done, turns):
            sums = list(sums)
            for turn in range(turns):
                entry = list_ref[done + turns * step + turn]
                for group in range(groups):
                    code = meta_ref[entry + group]
                    base = code >> CODE_SHIFT
                    back = code & (LANES - 1)
                    mask = lane >= ((-jnp.broadcast_to(code, (2 * slots, LANES))) & (LANES - 1)).astype(MASK)
                    piece = [pairs_ref[base + step_] for step_ in range(halves + 1)]
                    for part in range(halves):
                        mixed = jnp.where(mask, piece[part], piece[part + 1])
                        turned = pltpu.roll(mixed, back, 1).astype(jnp.float32)
                        for side in range(2):
                            sums[group * parts + side * halves + part] += turned[side * slots : (side + 1) * slots]
            return tuple(sums)

        zero = tuple(jnp.zeros((slots, LANES), jnp.float32) for _ in range(groups * parts))
        sums, done = zero, 0
        for turns in TURNS[:-1]:
            steps = (count - done) // turns
            sums = lax.fori_loop(0, steps, functools.partial(add, done=done, turns=turns), sums)
            done = done + steps * turns
        turns = TURNS[-1]
        sums = lax.fori_loop(0, (count - done + turns - 1) // turns, functools.partial(add, done=done, turns=turns), sums)
        for group in range(groups):
            for part in range(parts):
                sums_ref[tile, group, :, part * LANES : (part + 1) * LANES] = sums[group * parts + part].astype(jnp.bfloat16)
        pltpu.make_async_copy(sums_ref.at[tile], out_ref.at[tile], out_sems.at[tile]).start()
        return carry

    lax.fori_loop(0, tiles, one_tile, 0)
    for tile in range(tiles):
        pltpu.make_async_copy(sums_ref.at[tile], out_ref.at[tile], out_sems.at[tile]).wait()


def image_kernel(off_ref, stacked_ref, interp_ref, amp_ref, *refs, scale):
    *out_refs, image_ref = refs
    sources, groups, slots, window = stacked_ref.shape
    rows, pixels = out_refs[0].shape
    pixels = pixels // groups
    for group in range(groups):
        stacked = stacked_ref[:, group].reshape(sources * slots, window)
        depth = lax.dot_general(interp_ref[group], stacked, (((1,), (1,)), ((), ())), preferred_element_type=jnp.float32)
        high = depth.astype(jnp.bfloat16)
        low = (depth - high.astype(jnp.float32)).astype(jnp.bfloat16)
        amp = amp_ref[group]
        image = jnp.dot(high, amp, preferred_element_type=jnp.float32) + jnp.dot(low, amp, preferred_element_type=jnp.float32)
        image_ref[:, group * pixels : (group + 1) * pixels] = image * scale
    for apart, ref in enumerate(out_refs):
        ref[...] = image_ref[pl.ds(pl.multiple_of((off_ref[0] ^ apart) * rows, rows), rows), :].astype(ref.dtype)


def join_kernel(off_ref, *refs):
    out_ref = refs[-1]
    for apart, ref in enumerate(refs[:-1]):
        width = ref.shape[1]
        start = pl.multiple_of((off_ref[0] ^ apart) * width, LANES)
        out_ref[:, pl.ds(start, width)] = ref[...].astype(out_ref.dtype)


def ring_pairs(step):
    return [(z, (z + step) % 4) for z in range(4)]


def local(shot_traces, assign, aperture, band, interp, amp):
    blocks, samples = shot_traces.shape[1], shot_traces.shape[3]
    per_off, all_groups = band.shape
    offs = blocks // per_off
    groups = all_groups // offs
    tiles = lax.axis_size("x") * lax.axis_size("y")
    window, depth = interp.shape[1], interp.shape[2]
    pixels = amp.shape[2]
    chunks = samples // LANES
    zh, core, zl = lax.axis_index("zh"), lax.axis_index("core"), lax.axis_index("zl")
    z = zh * 2 + zl
    off = zh * 2 + core
    swap = [(0, 1), (1, 0)]

    smem = pl.BlockSpec(memory_space=pltpu.SMEM)
    vmem = pl.BlockSpec(memory_space=pltpu.VMEM)
    anywhere = pl.BlockSpec(memory_space=pl.ANY)

    pitch = chunks - window // LANES // 2 + 1
    sent, row = pl.pallas_call(
        functools.partial(prepare_kernel, offs=offs, pitch=pitch),
        out_shape=[
            pltpu.VMEM((blocks + 1, chunks, LANES), jnp.bfloat16),
            jax.ShapeDtypeStruct((offs * tiles, LANES), jnp.int32),
        ],
        in_specs=[smem] + [anywhere] * 4,
        out_specs=[vmem, anywhere],
        scratch_shapes=[
            pltpu.VMEM((blocks * chunks, LANES), jnp.float32),
            pltpu.VMEM((blocks, samples), jnp.bfloat16),
            pltpu.SMEM((assign.shape[2], per_off), jnp.int32),
            pltpu.SMEM((per_off, all_groups), jnp.int32),
            pltpu.SMEM((1, per_off), jnp.int32),
            pltpu.VMEM((offs * tiles, LANES), jnp.int32),
            pltpu.SemaphoreType.DMA((5,)),
        ],
        name="prepare_traces",
    )(off.reshape(1), *map(in_hbm, (shot_traces[0, :, 0, :], jnp.transpose(assign[:, 0, :]), band, jnp.transpose(aperture))))
    steps = (1, 3, 2)
    ring = [lax.ppermute(sent, ("zh", "zl"), ring_pairs(step)) for step in steps]

    meta = lax.all_to_all(row, ("core",) + PLANE, 0, 0, tiled=True)

    *ring, meta = lax.optimization_barrier((*ring, meta))
    column = [sent, *ring]
    pieces = column + [lax.ppermute(piece, "core", swap) for piece in column]
    tables = [meta.reshape(-1), lax.ppermute(meta, "zh", swap).reshape(-1)]
    pairs = pl.pallas_call(
        functools.partial(
            place_kernel, pieces=len(pieces), blocks=blocks, chunks=chunks, per_off=per_off, tiles=tiles, groups=groups, window=window
        ),
        out_shape=pltpu.VMEM(((blocks + 1) * pitch, 2 * SUB, LANES), jnp.bfloat16),
        in_specs=[smem, smem] + [vmem] * len(pieces),
        out_specs=vmem,
        scratch_shapes=[
            pltpu.VMEM((len(pieces), blocks + 1, chunks, LANES), jnp.bfloat16),
            pltpu.VMEM((2, (chunks + 1) * SUB, LANES), jnp.float32),
            pltpu.VMEM((len(pieces), LANES), jnp.int32),
            pltpu.SMEM((len(pieces), LANES), jnp.int32),
            pltpu.SemaphoreType.DMA((len(pieces) + 1,)),
        ],
        compiler_params=pltpu.CompilerParams(vmem_limit_bytes=VMEM_BYTES),
        name="place_traces",
    )(z.reshape(1), core.reshape(1), *map(in_vmem, pieces))
    stacked = pl.pallas_call(
        functools.partial(stack_kernel, blocks=blocks, chunks=chunks, per_off=per_off, tiles=tiles, groups=groups, window=window),
        out_shape=jax.ShapeDtypeStruct((tiles, groups, SUB, window), jnp.bfloat16),
        in_specs=[smem, anywhere, anywhere, vmem],
        out_specs=anywhere,
        scratch_shapes=[
            pltpu.VMEM((tiles, groups, SUB, window), jnp.bfloat16),
            pltpu.SMEM((2 * offs * tiles * LANES,), jnp.int32),
            pltpu.SMEM((blocks + TURNS[-1] - 1,), jnp.int32),
            pltpu.SemaphoreType.DMA((2,)),
            pltpu.SemaphoreType.DMA((tiles,)),
        ],
        compiler_params=pltpu.CompilerParams(vmem_limit_bytes=VMEM_BYTES),
        name="stack_windows",
    )(z.reshape(1), *map(in_vmem, tables), in_vmem(pairs))

    arrived = lax.all_to_all(stacked, PLANE, 0, 0, tiled=True)

    interp_here = lax.dynamic_slice_in_dim(jnp.swapaxes(interp, 1, 2), off * groups, groups, 0)
    amp_here = lax.dynamic_slice_in_dim(amp, off * groups, groups, 0)
    strip = (depth // offs, groups * pixels)
    own, beside, far, across = pl.pallas_call(
        functools.partial(image_kernel, scale=1.0 / math.sqrt(blocks)),
        out_shape=[pltpu.VMEM(strip, jnp.float32)] + [pltpu.VMEM(strip, jnp.bfloat16)] * 3,
        in_specs=[smem, vmem, vmem, vmem],
        out_specs=[vmem] * 4,
        scratch_shapes=[pltpu.VMEM((depth, groups * pixels), jnp.float32)],
        name="image_groups",
    )(off.reshape(1), in_vmem(arrived), in_vmem(interp_here), in_vmem(amp_here))

    far, across, beside = (
        lax.ppermute(strip, OFF, [(index, index ^ apart) for index in range(offs)])
        for apart, strip in ((2, far), (3, across), (1, beside))
    )
    return pl.pallas_call(
        join_kernel,
        out_shape=jax.ShapeDtypeStruct((depth // offs, offs * groups * pixels), jnp.float32),
        in_specs=[smem] + [vmem] * 4,
        out_specs=vmem,
        name="join_groups",
    )(off.reshape(1), *map(in_vmem, (own, beside, far, across)))


def solution(mesh):
    fine = Mesh(mesh.devices.reshape(2, 2, 4, 4, 2), EVERY)
    placed = (
        P(OFF, None, IMG, None),
        P(OFF, IMG, None),
        P(OFF, IMG),
        P(OFF, IMG),
        P(IMG, None, None),
        P(IMG, None, None),
    )
    return jax.shard_map(local, mesh=fine, in_specs=placed, out_specs=P(OFF, IMG), check_vma=False)
```

```python
import functools
import math

import jax
import jax.numpy as jnp
from jax import lax
from jax.experimental import pallas as pl
from jax.experimental.pallas import tpu as pltpu
from jax.sharding import Mesh, PartitionSpec as P

LANES = 128
SUB = 8
OFF = ("zh", "core")
PLANE = ("x", "y")
IMG = ("x", "y", "zl")
EVERY = OFF + IMG
CODE_SHIFT = 7
TURNS = (16, 8)
MASK = jnp.int16
VMEM_BYTES = 24 * 2**20


def in_hbm(array):
    return pltpu.with_memory_space_constraint(array, pltpu.HBM)


def in_vmem(array):
    return pltpu.with_memory_space_constraint(array, pltpu.VMEM)


def code_rows(off_ref, band_ref, aperture_ref, meta_ref, *, offs, owned, pitch):
    groups = band_ref.shape[1] // offs
    spot = lax.broadcasted_iota(jnp.int32, (SUB, LANES), 1)
    line = lax.broadcasted_iota(jnp.int32, (SUB, LANES), 0)
    here = jnp.zeros((SUB, LANES), jnp.int32)
    first = jnp.zeros((SUB, LANES), jnp.int32)
    count = 0
    for within in range(owned):
        inside = aperture_ref[0, within]
        turn = owned + inside * (count - owned)
        count = count + inside
        here = jnp.where(spot // groups == turn, (off_ref[0] * owned + within) * pitch, here)
        for group in range(groups):
            values = jnp.zeros((SUB, LANES), jnp.int32)
            for owner in range(offs):
                values = jnp.where(line == owner, band_ref[within, owner * groups + group], values)
            first = jnp.where(spot == turn * groups + group, values, first)
    flags = jnp.where(spot == owned * groups, count, (offs * owned * pitch) << CODE_SHIFT)
    code = ((here + (first >> 7)) << CODE_SHIFT) | ((-first) & (LANES - 1))
    block = jnp.where(spot < owned * groups, code, flags)
    tiles = meta_ref.shape[0] // offs
    for core in range(2):
        row = jnp.where(line % 2 == 0, block[core : core + 1], block[2 + core : 3 + core])
        for start in range(0, 2 * tiles, SUB):
            meta_ref[core * 2 * tiles + start : core * 2 * tiles + start + SUB] = row


def prepare_kernel(off_ref, *refs, offs, pitch):
    *sources, out_ref, sent_ref, rows_ref, traces_ref, assign_ref, band_ref, aperture_ref, meta_ref, sems = refs
    fetch, *smalls = [
        pltpu.make_async_copy(source, held, sems.at[index])
        for index, (source, held) in enumerate(zip(sources, (traces_ref, assign_ref, band_ref, aperture_ref)))
    ]
    for copy in (fetch, *smalls):
        copy.start()
    for copy in smalls:
        copy.wait()
    code_rows(off_ref, band_ref, aperture_ref, meta_ref, offs=offs, owned=assign_ref.shape[1], pitch=pitch)
    send = pltpu.make_async_copy(meta_ref, sent_ref, sems.at[4])
    send.start()
    fetch.wait()
    blocks, samples = traces_ref.shape
    chunks = samples // LANES
    lane = lax.broadcasted_iota(jnp.int32, (blocks, LANES), 1)
    before = jnp.zeros((blocks, LANES), jnp.float32)
    for chunk in range(chunks):
        here = traces_ref[:, chunk * LANES : (chunk + 1) * LANES].astype(jnp.float32)
        turned = pltpu.roll(here, 1, 1)
        rows_ref[pl.ds(chunk, blocks, stride=chunks), :] = here - 0.9 * jnp.where(lane == 0, before, turned)
        before = turned
    for block in range(blocks):
        out_ref[block] = rows_ref[block * chunks : (block + 1) * chunks].astype(out_ref.dtype)
    slots, owned = assign_ref.shape
    spot = lax.broadcasted_iota(jnp.int32, (chunks, LANES), 1)
    codes = jnp.zeros((chunks, LANES), jnp.float32)
    for slot in range(slots):
        for within in range(owned):
            codes = jnp.where(spot == slot * owned + within, assign_ref[slot, within].astype(jnp.float32), codes)
    out_ref[blocks] = codes.astype(out_ref.dtype)
    send.wait()


def spot_of(piece, z, core):
    from_z = (z - ((piece % 4) ^ (piece % 4 >> 1))) & 3
    return (from_z >> 1) * 4 + (core ^ (piece // 4)) * 2 + (from_z & 1)


def place_kernel(z_ref, core_ref, *refs, pieces, blocks, chunks, per_off, tiles, groups, window):
    piece_refs = refs[:pieces]
    pairs_ref, traces_ref, rows_ref, words_ref, codes_ref, sems = refs[pieces:]
    slots = SUB
    parts = window // LANES
    halves = parts // 2
    pitch = chunks - halves + 1
    z, core = z_ref[0], core_ref[0]
    for piece in range(pieces):
        words_ref[piece : piece + 1] = piece_refs[piece][blocks, 0:1, :].astype(jnp.float32).astype(jnp.int32)
    fetch = pltpu.make_async_copy(words_ref, codes_ref, sems.at[pieces])
    fetch.start()
    copies = [
        pltpu.make_async_copy(piece_refs[piece], traces_ref.at[spot_of(piece, z, core)], sems.at[piece])
        for piece in range(pieces)
    ]
    for copy in copies:
        copy.start()
    lane = lax.broadcasted_iota(jnp.int32, (2 * slots, LANES), 1).astype(MASK)
    zeros = jnp.zeros((2 * slots, LANES), jnp.bfloat16)
    for step in range(pitch):
        pairs_ref[blocks * pitch + step] = zeros
    for turn in range(2):
        rows_ref[turn, chunks * slots :] = jnp.zeros((slots, LANES), jnp.float32)
    for copy in copies:
        copy.wait()
    fetch.wait()

    def place(owner, carry):
        steps = [(z - (owner >> 1) * 2 - half) & 3 for half in range(2)]
        held = [(core ^ (owner & 1)) * 4 + (step ^ (step >> 1)) for step in steps]
        for within in range(per_off):
            block = owner * per_off + within
            turn = within % 2
            for slot in range(slots):
                source = codes_ref[held[slot // 4], (slot % 4) * per_off + within] * 2 + slot // 4
                rows_ref[turn, pl.ds(slot, chunks, stride=slots), :] = traces_ref[source, block].astype(jnp.float32)
            start = block * pitch
            for step in range(pitch):
                near = rows_ref[turn, step * slots : (step + 1) * slots]
                far = rows_ref[turn, (step + halves) * slots : (step + halves + 1) * slots]
                pairs_ref[start + step] = jnp.concatenate([near, far], axis=0).astype(jnp.bfloat16)
        return carry

    lax.fori_loop(0, blocks // per_off, place, 0)


def stack_kernel(z_ref, near_ref, far_ref, pairs_ref, out_ref, sums_ref, meta_ref, list_ref, sems, out_sems, *, blocks, chunks, per_off, tiles, groups, window):
    z = z_ref[0]
    span = near_ref.shape[0]
    fetches = [
        pltpu.make_async_copy(ref, meta_ref.at[pl.ds(index * span, span)], sems.at[index])
        for index, ref in enumerate((near_ref, far_ref))
    ]
    for table in fetches:
        table.start()
    slots = SUB
    parts = window // LANES
    halves = parts // 2
    pitch = chunks - halves + 1
    lane = lax.broadcasted_iota(jnp.int32, (2 * slots, LANES), 1).astype(MASK)
    for table in fetches:
        table.wait()

    def one_tile(tile, carry):
        count = 0
        for owner in range(blocks // per_off):
            row = owner // 2 * span + ((owner % 2 * tiles + tile) * 2 + (z >> 1)) * LANES
            for turn in range(per_off):
                list_ref[count + turn] = row + turn * groups
            count = count + meta_ref[row + per_off * groups]
        for more in range(TURNS[-1] - 1):
            list_ref[count + more] = per_off * groups + per_off

        def add(step, sums, done, turns):
            sums = list(sums)
            for turn in range(turns):
                entry = list_ref[done + turns * step + turn]
                for group in range(groups):
                    code = meta_ref[entry + group]
                    base = code >> CODE_SHIFT
                    back = code & (LANES - 1)
                    mask = lane >= ((-jnp.broadcast_to(code, (2 * slots, LANES))) & (LANES - 1)).astype(MASK)
                    piece = [pairs_ref[base + step_] for step_ in range(halves + 1)]
                    for part in range(halves):
                        mixed = jnp.where(mask, piece[part], piece[part + 1])
                        turned = pltpu.roll(mixed, back, 1).astype(jnp.float32)
                        for side in range(2):
                            sums[group * parts + side * halves + part] += turned[side * slots : (side + 1) * slots]
            return tuple(sums)

        zero = tuple(jnp.zeros((slots, LANES), jnp.float32) for _ in range(groups * parts))
        sums, done = zero, 0
        for turns in TURNS[:-1]:
            steps = (count - done) // turns
            sums = lax.fori_loop(0, steps, functools.partial(add, done=done, turns=turns), sums)
            done = done + steps * turns
        turns = TURNS[-1]
        sums = lax.fori_loop(0, (count - done + turns - 1) // turns, functools.partial(add, done=done, turns=turns), sums)
        for group in range(groups):
            for part in range(parts):
                sums_ref[tile, group, :, part * LANES : (part + 1) * LANES] = sums[group * parts + part].astype(jnp.bfloat16)
        pltpu.make_async_copy(sums_ref.at[tile], out_ref.at[tile], out_sems.at[tile]).start()
        return carry

    lax.fori_loop(0, tiles, one_tile, 0)
    for tile in range(tiles):
        pltpu.make_async_copy(sums_ref.at[tile], out_ref.at[tile], out_sems.at[tile]).wait()


def image_kernel(off_ref, stacked_ref, interp_ref, amp_ref, *refs, scale):
    *out_refs, image_ref = refs
    sources, groups, slots, window = stacked_ref.shape
    rows, pixels = out_refs[0].shape
    pixels = pixels // groups
    for group in range(groups):
        stacked = stacked_ref[:, group].reshape(sources * slots, window)
        depth = lax.dot_general(interp_ref[group], stacked, (((1,), (1,)), ((), ())), preferred_element_type=jnp.float32)
        high = depth.astype(jnp.bfloat16)
        low = (depth - high.astype(jnp.float32)).astype(jnp.bfloat16)
        amp = amp_ref[group]
        image = jnp.dot(high, amp, preferred_element_type=jnp.float32) + jnp.dot(low, amp, preferred_element_type=jnp.float32)
        image_ref[:, group * pixels : (group + 1) * pixels] = image * scale
    for apart, ref in enumerate(out_refs):
        ref[...] = image_ref[pl.ds(pl.multiple_of((off_ref[0] ^ apart) * rows, rows), rows), :].astype(ref.dtype)


def join_kernel(off_ref, *refs):
    out_ref = refs[-1]
    for apart, ref in zip((0, 2, 3, 1), refs[:-1]):
        width = ref.shape[1]
        start = pl.multiple_of((off_ref[0] ^ apart) * width, LANES)
        out_ref[:, pl.ds(start, width)] = ref[...].astype(out_ref.dtype)


def ring_pairs(step):
    return [(z, (z + step) % 4) for z in range(4)]


def local(shot_traces, assign, aperture, band, interp, amp):
    blocks, samples = shot_traces.shape[1], shot_traces.shape[3]
    per_off, all_groups = band.shape
    offs = blocks // per_off
    groups = all_groups // offs
    tiles = lax.axis_size("x") * lax.axis_size("y")
    window, depth = interp.shape[1], interp.shape[2]
    pixels = amp.shape[2]
    chunks = samples // LANES
    zh, core, zl = lax.axis_index("zh"), lax.axis_index("core"), lax.axis_index("zl")
    z = zh * 2 + zl
    off = zh * 2 + core
    swap = [(0, 1), (1, 0)]

    smem = pl.BlockSpec(memory_space=pltpu.SMEM)
    vmem = pl.BlockSpec(memory_space=pltpu.VMEM)
    anywhere = pl.BlockSpec(memory_space=pl.ANY)

    pitch = chunks - window // LANES // 2 + 1
    sent, row = pl.pallas_call(
        functools.partial(prepare_kernel, offs=offs, pitch=pitch),
        out_shape=[
            pltpu.VMEM((blocks + 1, chunks, LANES), jnp.bfloat16),
            jax.ShapeDtypeStruct((offs * tiles, LANES), jnp.int32),
        ],
        in_specs=[smem] + [anywhere] * 4,
        out_specs=[vmem, anywhere],
        scratch_shapes=[
            pltpu.VMEM((blocks * chunks, LANES), jnp.float32),
            pltpu.VMEM((blocks, samples), jnp.bfloat16),
            pltpu.SMEM((assign.shape[2], per_off), jnp.int32),
            pltpu.SMEM((per_off, all_groups), jnp.int32),
            pltpu.SMEM((1, per_off), jnp.int32),
            pltpu.VMEM((offs * tiles, LANES), jnp.int32),
            pltpu.SemaphoreType.DMA((5,)),
        ],
        name="prepare_traces",
    )(off.reshape(1), *map(in_hbm, (shot_traces[0, :, 0, :], jnp.transpose(assign[:, 0, :]), band, jnp.transpose(aperture))))
    steps = (1, 3, 2)
    ring = [lax.ppermute(sent, ("zh", "zl"), ring_pairs(step)) for step in steps]

    meta = lax.all_to_all(row, ("core",) + PLANE, 0, 0, tiled=True)

    *ring, meta = lax.optimization_barrier((*ring, meta))
    column = [sent, *ring]
    pieces = column + [lax.ppermute(piece, "core", swap) for piece in column]
    tables = [meta.reshape(-1), lax.ppermute(meta, "zh", swap).reshape(-1)]
    pairs = pl.pallas_call(
        functools.partial(
            place_kernel, pieces=len(pieces), blocks=blocks, chunks=chunks, per_off=per_off, tiles=tiles, groups=groups, window=window
        ),
        out_shape=pltpu.VMEM(((blocks + 1) * pitch, 2 * SUB, LANES), jnp.bfloat16),
        in_specs=[smem, smem] + [vmem] * len(pieces),
        out_specs=vmem,
        scratch_shapes=[
            pltpu.VMEM((len(pieces), blocks + 1, chunks, LANES), jnp.bfloat16),
            pltpu.VMEM((2, (chunks + 1) * SUB, LANES), jnp.float32),
            pltpu.VMEM((len(pieces), LANES), jnp.int32),
            pltpu.SMEM((len(pieces), LANES), jnp.int32),
            pltpu.SemaphoreType.DMA((len(pieces) + 1,)),
        ],
        compiler_params=pltpu.CompilerParams(vmem_limit_bytes=VMEM_BYTES),
        name="place_traces",
    )(z.reshape(1), core.reshape(1), *map(in_vmem, pieces))
    stacked = pl.pallas_call(
        functools.partial(stack_kernel, blocks=blocks, chunks=chunks, per_off=per_off, tiles=tiles, groups=groups, window=window),
        out_shape=jax.ShapeDtypeStruct((tiles, groups, SUB, window), jnp.bfloat16),
        in_specs=[smem, anywhere, anywhere, vmem],
        out_specs=anywhere,
        scratch_shapes=[
            pltpu.VMEM((tiles, groups, SUB, window), jnp.bfloat16),
            pltpu.SMEM((2 * offs * tiles * LANES,), jnp.int32),
            pltpu.SMEM((blocks + TURNS[-1] - 1,), jnp.int32),
            pltpu.SemaphoreType.DMA((2,)),
            pltpu.SemaphoreType.DMA((tiles,)),
        ],
        compiler_params=pltpu.CompilerParams(vmem_limit_bytes=VMEM_BYTES),
        name="stack_windows",
    )(z.reshape(1), *map(in_vmem, tables), in_vmem(pairs))

    arrived = lax.all_to_all(stacked, PLANE, 0, 0, tiled=True)

    interp_here = lax.dynamic_slice_in_dim(jnp.swapaxes(interp, 1, 2), off * groups, groups, 0)
    amp_here = lax.dynamic_slice_in_dim(amp, off * groups, groups, 0)
    strip = (depth // offs, groups * pixels)
    own, beside, far, across = pl.pallas_call(
        functools.partial(image_kernel, scale=1.0 / math.sqrt(blocks)),
        out_shape=[pltpu.VMEM(strip, jnp.float32)] + [pltpu.VMEM(strip, jnp.bfloat16)] * 3,
        in_specs=[smem, vmem, vmem, vmem],
        out_specs=[vmem] * 4,
        scratch_shapes=[pltpu.VMEM((depth, groups * pixels), jnp.float32)],
        name="image_groups",
    )(off.reshape(1), in_vmem(arrived), in_vmem(interp_here), in_vmem(amp_here))

    far, across, beside = (
        lax.ppermute(strip, OFF, [(index, index ^ apart) for index in range(offs)])
        for apart, strip in ((2, far), (3, across), (1, beside))
    )
    return pl.pallas_call(
        join_kernel,
        out_shape=jax.ShapeDtypeStruct((depth // offs, offs * groups * pixels), jnp.float32),
        in_specs=[smem] + [vmem] * 4,
        out_specs=vmem,
        name="join_groups",
    )(off.reshape(1), *map(in_vmem, (own, far, across, beside)))


def solution(mesh):
    fine = Mesh(mesh.devices.reshape(2, 2, 4, 4, 2), EVERY)
    placed = (
        P(OFF, None, IMG, None),
        P(OFF, IMG, None),
        P(OFF, IMG),
        P(OFF, IMG),
        P(IMG, None, None),
        P(IMG, None, None),
    )
    return jax.shard_map(local, mesh=fine, in_specs=placed, out_specs=P(OFF, IMG), check_vma=False)
```
